256 devices in a mesh: bulk: 16 (over x, y), wide: 16 (over z, core).
Axes of the slice: x: 4, y: 4, z: 8, core: 2. Of those that a mesh axis runs over, the one named last changes fastest.
Arguments:
- particle_cell: int32 [256, 512], P(('bulk', 'wide')), may hold values from 0 to 4095
- particle_frac: float32 [256, 512], P(('bulk', 'wide')), may hold values from 0 to 1
- particle_mass: float32 [256, 512], P(('bulk', 'wide')), may hold values from 0.5 to 2
- particle_vel: float32 [3, 256, 512], P(None, ('bulk', 'wide')), may hold values from -6 to 6
- node_cell: int32 [4096, 256], P(('bulk', 'wide')), may hold values from 0 to 4095
- node_body: int32 [4096, 256], P(('bulk', 'wide')), may hold values from 0 to 511
- node_count: int32 [4096], P(('bulk', 'wide')), may hold values from 1 to 256, as said below
- node_pos: float32 [3, 4096, 256], P(None, ('bulk', 'wide')), may hold values from -4 to 4
- body_state: float32 [12, 131072], P(None, ('bulk', 'wide')), may hold values from -4 to 4, as said below
- body_vel: float32 [12, 131072], P(None, ('bulk', 'wide')), may hold values from -3 to 3
- body_mass: float32 [131072], P(('bulk', 'wide')), may hold values from 1 to 4
- touch_body: int32 [4096, 128], P(('bulk', 'wide')), may hold values from 0 to 511
- touch_pos: float32 [3, 4096, 128], P(None, ('bulk', 'wide')), may hold values from -4 to 4
Outputs:
- body_next: float32 [12, 131072], P(None, ('bulk', 'wide'))
- grid_velocity: float32 [3, 256, 16, 256], P(None, 'bulk', 'wide')
- touch_point: float32 [3, 4096, 128], P(None, ('bulk', 'wide'))
The draws below stay inside these ranges and needn't reach their ends.
Inputs may be any that keep to these rules, and one draw needn't show every extreme that they name: `node_count`: for each device and owner, the live node slots; every draw has an owner that receives 256 live rows from every device. `body_state`: rows 3 to 11 hold a 3 x 3 matrix within 0.3 of the identity in every entry; rows 0 to 2 within -4 to 4. `touch_body`: every device lists 128 touch slots for every owner.
All inputs are finite; a program needn't handle non-finite values.
Results may differ from the reference program's by a relative error of at most 0.0018.
Values sent between devices are 32-bit elements; how exact they have to be, the bound alone decides.
No kernel may reach another device: no remote copies, remote signals or barrier semaphores. Data moves between devices by JAX's collectives and lax.ppermute only.
A program may use at most 64 MiB of HBM per device.

```python
import math
import jax
import jax.numpy as jnp
from jax import lax

LAYERS = 16
COLUMNS = 256
BR = 1
PPB = 512
BOD_DEV = 512
CAP = 256
TCAP = 128
BODIES = 131072
N_BULK = 16
N_WIDE = 16
DEVICES = 256


def draw_node_count(key, part):
    first_key, second_key, third_key = jax.random.split(jax.random.fold_in(key, 11), 3)
    first = jax.random.randint(first_key, (DEVICES * N_WIDE,), 1, CAP + 1)
    second = jax.random.randint(second_key, (DEVICES * N_WIDE,), 1, CAP + 1)
    counts = jnp.minimum(first, second)
    busiest = jax.random.randint(third_key, (), 0, N_WIDE)
    owners = jnp.arange(DEVICES * N_WIDE, dtype=jnp.int32) % N_WIDE
    return jnp.where(owners == busiest, CAP, counts).astype(jnp.int32)


def draw_body_state(key, part):
    first_key, second_key = jax.random.split(jax.random.fold_in(key, 23), 2)
    shifts = jnp.clip(1.5 * jax.random.normal(first_key, (3, BODIES), jnp.float32), -4.0, 4.0)
    noise = jnp.clip(0.15 * jax.random.normal(second_key, (9, BODIES), jnp.float32), -0.3, 0.3)
    identity = jnp.eye(3, dtype=jnp.float32).reshape(9, 1)
    return jnp.concatenate([shifts, identity + noise], axis=0).astype(jnp.float32)


def with_ends(result, rng, least, top_value):
    spot = [jax.random.randint(jax.random.fold_in(rng, axis), (), 0, length) for axis, length in enumerate(result.shape)]
    longest = result.shape.index(max(result.shape))
    neighbour = spot[:longest] + [(spot[longest] + 1) % result.shape[longest]] + spot[longest + 1:]
    return result.at[tuple(spot)].set(least).at[tuple(neighbour)].set(top_value)


def block_levels(stream_key, dims, pieces, smallest, largest):
    def one(axis_at, shards_of):
        steps = jax.random.uniform(jax.random.fold_in(jax.random.fold_in(stream_key, 6), axis_at), (shards_of,), jnp.float32, smallest / len(pieces), largest / len(pieces))
        return jnp.repeat(jnp.exp(steps), dims[axis_at] // shards_of).reshape((-1,) + (1,) * (len(dims) - axis_at - 1))

    level = one(*pieces[0])
    for cut in pieces[1:]:
        level = level * one(*cut)
    return level


def bell_draw(key, extent, spread, most, pieces=(), held_as=jnp.bfloat16):
    values = jax.random.normal(key, extent, jnp.float32) * spread
    if len(pieces) > 0:
        values = block_levels(key, extent, pieces, -0.22, 0.18) * values
    return jnp.clip(values, min=-most, max=most).astype(held_as)


def setup_inputs(seed: int = 0) -> dict:
    arg_keys = jax.random.split(jax.random.key(seed), 14)
    return {
        "particle_cell": with_ends(jax.random.randint(arg_keys[0], (DEVICES * BR, PPB), 0, LAYERS * COLUMNS), jax.random.fold_in(arg_keys[0], 1), 0, (LAYERS * COLUMNS) - 1).astype(jnp.int32),
        "particle_frac": jnp.clip(1.0 * jax.random.uniform(arg_keys[1], (DEVICES * BR, PPB), jnp.float32) ** block_levels(arg_keys[1], (DEVICES * BR, PPB), ((0, 256),), -0.2, 0.2), 0.0, 1.0),
        "particle_mass": jnp.clip(jnp.exp(math.log(2.0) - 1.3862944 * jax.random.uniform(arg_keys[2], (DEVICES * BR, PPB), jnp.float32) ** block_levels(arg_keys[2], (DEVICES * BR, PPB), ((0, 256),), -0.2, 0.2)), 0.5, 2.0),
        "particle_vel": bell_draw(arg_keys[3], (3, DEVICES * BR, PPB), 1.0, 6.0, ((1, 256),), jnp.float32),
        "node_cell": with_ends(jax.random.randint(arg_keys[4], (DEVICES * N_WIDE, CAP), 0, LAYERS * BR * COLUMNS), jax.random.fold_in(arg_keys[4], 1), 0, (LAYERS * BR * COLUMNS) - 1).astype(jnp.int32),
        "node_body": with_ends(jax.random.randint(arg_keys[5], (DEVICES * N_WIDE, CAP), 0, BOD_DEV), jax.random.fold_in(arg_keys[5], 1), 0, BOD_DEV - 1).astype(jnp.int32),
        "node_count": draw_node_count(jax.random.fold_in(arg_keys[13], 71), 0),
        "node_pos": bell_draw(arg_keys[7], (3, DEVICES * N_WIDE, CAP), 1.0, 4.0, ((1, 256),), jnp.float32),
        "body_state": draw_body_state(jax.random.fold_in(arg_keys[13], 71), 0),
        "body_vel": bell_draw(arg_keys[9], (12, BODIES), 0.5, 3.0, ((1, 256),), jnp.float32),
        "body_mass": jnp.clip(jnp.exp(math.log(4.0) - 1.3862944 * jax.random.uniform(arg_keys[10], (BODIES,), jnp.float32) ** block_levels(arg_keys[10], (BODIES,), ((0, 256),), -0.2, 0.2)), 1.0, 4.0),
        "touch_body": with_ends(jax.random.randint(arg_keys[11], (DEVICES * N_WIDE, TCAP), 0, BOD_DEV), jax.random.fold_in(arg_keys[11], 1), 0, BOD_DEV - 1).astype(jnp.int32),
        "touch_pos": bell_draw(arg_keys[12], (3, DEVICES * N_WIDE, TCAP), 1.0, 4.0, ((1, 256),), jnp.float32),
    }


stiffness = 0.05
gravity_pull = -0.5


def brick_values(cells, fractions, masses, velocities):
    lower = 1.0 - fractions
    upper = fractions
    moments = masses[None] * velocities
    stacked = jnp.concatenate([(masses * lower)[None], moments * lower[None], (masses * upper)[None], moments * upper[None]], axis=0)
    return stacked.astype(jnp.bfloat16)


def extend_brick(totals):
    extended = jnp.zeros((4, (LAYERS + 1) * COLUMNS), jnp.float32)
    extended = extended.at[:, :LAYERS * COLUMNS].add(totals[:4])
    return extended.at[:, COLUMNS:].add(totals[4:])


def brick_sums(operands):
    cells, fractions, masses, velocities = operands
    values = brick_values(cells, fractions, masses, velocities).astype(jnp.float32)
    totals = jnp.zeros((8, LAYERS * COLUMNS), jnp.float32).at[:, cells].add(values)
    return extend_brick(totals)


def solve_nine(matrix, right_hand):
    matrix_rows = [matrix[number] for number in range(9)]
    right_side = [right_hand[number] for number in range(9)]
    for column in range(9):
        for lower_row in range(column + 1, 9):
            factor = matrix_rows[lower_row][column] / matrix_rows[column][column]
            matrix_rows[lower_row] = matrix_rows[lower_row] - factor * matrix_rows[column]
            right_side[lower_row] = right_side[lower_row] - factor * right_side[column]
    answer = [None] * 9
    for column in reversed(range(9)):
        residual = right_side[column]
        for column_after in range(column + 1, 9):
            residual = residual - matrix_rows[column][column_after] * answer[column_after]
        answer[column] = residual / matrix_rows[column][column]
    return jnp.stack(answer)


def newton_step(states, velocities, masses, forces):
    highest = lax.Precision.HIGHEST
    batch_size = states.shape[1]
    identity = jnp.eye(3, dtype=jnp.float32)
    affine = states[3:].reshape(3, 3, batch_size)
    moved = states[:3] + velocities[:3] + forces[:3] / masses[None]
    strain = jnp.einsum("imb,jmb->ijb", affine, affine, precision=highest) - identity[:, :, None]
    restoring = 4.0 * jnp.einsum("imb,mjb->ijb", strain, affine, precision=highest)
    gram = jnp.einsum("mlb,mjb->ljb", affine, affine, precision=highest)
    first = identity[:, None, :, None, None] * gram[None, :, None, :, :]
    second = jnp.einsum("ilb,kjb->ijklb", affine, affine, precision=highest)
    third = strain[:, None, :, None, :] * identity[None, :, None, :, None]
    hessian = (4.0 * stiffness) * (first + second + third).reshape(9, 9, batch_size)
    hessian = hessian + masses[None, None] * jnp.eye(9, dtype=jnp.float32)[:, :, None]
    right_hand = masses[None] * velocities[3:] + forces[3:] - stiffness * restoring.reshape(9, batch_size)
    update = solve_nine(hessian, right_hand)
    return jnp.concatenate([moved, states[3:] + update], axis=0)


def place_points(picked, positions):
    affine = picked[3:].reshape((3, 3) + picked.shape[1:])
    return picked[:3] + jnp.einsum("ijst,jst->ist", affine, positions, precision=lax.Precision.HIGHEST)


def reference(particle_cell, particle_frac, particle_mass, particle_vel, node_cell, node_body, node_count, node_pos, body_state, body_vel, body_mass, touch_body, touch_pos):
    bulk_count = N_BULK
    wide_count = N_WIDE
    bricks = lax.map(brick_sums, (particle_cell, particle_frac, particle_mass, jnp.moveaxis(particle_vel, 1, 0)))
    bricks = bricks.reshape(bulk_count, wide_count, BR, 4, LAYERS + 1, COLUMNS)
    interior = bricks[:, :, :, :, :LAYERS]
    ghost_layer = bricks[:, :, :, :, LAYERS]
    interior = interior.at[1:, :, :, :, 0].add(ghost_layer[:-1])
    mass_grid = interior[:, :, :, 0]
    pull_vector = jnp.array([0.0, 0.0, gravity_pull], jnp.float32)
    velocity = interior[:, :, :, 1:] / (mass_grid[:, :, :, None] + 1.0) + pull_vector[None, None, None, :, None, None]
    layer_ids = jnp.arange(bulk_count, dtype=jnp.int32)[:, None] * LAYERS + jnp.arange(LAYERS, dtype=jnp.int32)[None]
    walls = (layer_ids == 0) | (layer_ids == bulk_count * LAYERS - 1)
    velocity = jnp.where(walls[:, None, None, None, :, None], jnp.float32(0.0), velocity)
    grid_velocity = jnp.transpose(velocity, (3, 0, 4, 1, 2, 5)).reshape(3, bulk_count * LAYERS, wide_count * BR, COLUMNS)
    cells_device = LAYERS * BR * COLUMNS
    mass_flat = jnp.transpose(mass_grid, (0, 1, 3, 2, 4)).reshape(bulk_count, wide_count, cells_device)
    velocity_flat = jnp.transpose(velocity, (0, 1, 3, 4, 2, 5)).reshape(bulk_count, wide_count, 3, cells_device)
    node_index = node_cell.reshape(bulk_count, wide_count, wide_count * CAP)
    node_mass = jnp.take_along_axis(mass_flat, node_index, axis=2)
    wide_index = jnp.broadcast_to(node_index[:, :, None], (bulk_count, wide_count, 3, wide_count * CAP))
    node_velocity = jnp.take_along_axis(velocity_flat, wide_index, axis=3)
    push = (node_mass[:, :, None] * node_velocity).reshape(bulk_count, wide_count, 3, wide_count, CAP)
    live = jnp.arange(CAP, dtype=jnp.int32)[None, None, None, :] < node_count.reshape(bulk_count, wide_count, wide_count)[:, :, :, None]
    push = jnp.where(live[:, :, None], push, jnp.float32(0.0))
    offsets = jnp.moveaxis(node_pos.reshape(3, bulk_count, wide_count, wide_count, CAP), 0, 2)
    outer = (push[:, :, :, None] * offsets[:, :, None]).reshape(bulk_count, wide_count, 9, wide_count, CAP)
    general = jnp.concatenate([push, outer], axis=2)
    row_base = (jnp.arange(bulk_count, dtype=jnp.int32)[:, None, None, None] * wide_count + jnp.arange(wide_count, dtype=jnp.int32)[None, None, :, None]) * BOD_DEV
    owners = row_base + node_body.reshape(bulk_count, wide_count, wide_count, CAP)
    forces = jnp.zeros((12, BODIES), jnp.float32).at[:, owners.reshape(-1)].add(jnp.moveaxis(general, 2, 0).reshape(12, -1))
    body_next = newton_step(body_state, body_vel, body_mass, forces)
    touched = row_base + touch_body.reshape(bulk_count, wide_count, wide_count, TCAP)
    picked = body_next[:, touched.reshape(-1)].reshape(12, bulk_count * wide_count * wide_count, TCAP)
    touch_point = place_points(picked, touch_pos)
    return body_next, grid_velocity, touch_point
```

```python
import functools

import jax
import jax.numpy as jnp
from jax import lax
from jax.experimental import pallas as pl
from jax.experimental.pallas import tpu as pltpu
from jax.sharding import PartitionSpec as P

LAYERS = 16
COLUMNS = 256
LANES = 128
STIFFNESS = 0.05
PULL = (0.0, 0.0, -0.5)
ROWS = 24
NODE_BODY, NODE_POS, TOUCH_BODY, TOUCH_POS = 6, 8, 14, 15
BACK = 8

f32, bf16, i32 = jnp.float32, jnp.bfloat16, jnp.int32
VMEM = pl.BlockSpec(memory_space=pltpu.VMEM)
SMEM = pl.BlockSpec(memory_space=pltpu.SMEM)


def iota(shape, dim):
    return lax.broadcasted_iota(i32, shape, dim)


def rows_dot(a, b):
    return lax.dot_general(a, b, (((1,), (1,)), ((), ())), preferred_element_type=f32)


def particles_kernel(cell_ref, frac_ref, mass_ref, vel_ref, total_ref, ghost_ref):
    cell = cell_ref[...]
    layer, column = cell >> 8, cell & 255
    frac, mass = frac_ref[...], mass_ref[...]
    lower = 1.0 - frac
    count = cell.shape[1]
    moments = [mass * vel_ref[i] for i in range(3)]
    low = [mass * lower] + [moment * lower for moment in moments]
    high = [mass * frac] + [moment * frac for moment in moments]
    rounded = lambda x: x.astype(bf16).astype(f32)
    layers = iota((LAYERS, count), 0)
    here, above = layers == layer, layers == layer + 1
    past = iota((8, count), 0)
    blocks = [jnp.where(here, rounded(x), 0.0) for x in low]
    blocks += [jnp.where(above, rounded(x), 0.0) for x in high]
    ghost = jnp.zeros((8, count), f32)
    for i, x in enumerate(high):
        ghost = jnp.where((past == i) & (layer == LAYERS - 1), rounded(x), ghost)
    left = jnp.concatenate(blocks + [ghost, jnp.zeros((8, count), f32)], axis=0).astype(bf16)
    table = jnp.where(iota((COLUMNS, count), 0) == column, 1.0, 0.0).astype(bf16)
    sums = rows_dot(left, table)
    half = 4 * LAYERS
    total_ref[...] = sums[:half] + sums[half : 2 * half]
    ghost_ref[...] = sums[2 * half : 2 * half + 8]


def lane_pick(row, index):
    table = jnp.broadcast_to(row, index.shape)
    return jnp.take_along_axis(table, index, axis=1, mode="promise_in_bounds")


def grid_kernel(
    bulk_ref, total_ref, ghost_ref, cell_ref, body_ref, count_ref, pos_ref, touch_ref, touch_pos_ref,
    velocity_ref, sent_ref,
):
    bulk, last = bulk_ref[0], bulk_ref[1]
    layers = iota((LAYERS, COLUMNS), 0)
    joins = (layers == 0) & (bulk > 0)
    wall = ((layers == 0) & (bulk == 0)) | ((layers == LAYERS - 1) & (bulk == last))
    sums = [
        total_ref[LAYERS * i : LAYERS * (i + 1)] + jnp.where(joins, ghost_ref[i : i + 1], 0.0)
        for i in range(4)
    ]
    mass = sums[0]
    push = []
    for i in range(3):
        velocity = jnp.where(wall, 0.0, sums[i + 1] / (mass + 1.0) + PULL[i])
        velocity_ref[i] = velocity
        push.append(mass * velocity)
    owners = cell_ref.shape[0]
    lanes = iota((owners, LANES), 1)
    counts = jnp.sum(
        jnp.where(iota((owners, owners), 0) == iota((owners, owners), 1), count_ref[...], 0),
        axis=1, keepdims=True,
    )

    def put(row, value):
        sent_ref[pl.ds(row, owners, stride=ROWS), :] = value

    for half in range(2):
        part = slice(half * LANES, (half + 1) * LANES)
        cell = cell_ref[:, part]
        key, index = cell >> 7, cell & (LANES - 1)
        found = [jnp.zeros((owners, LANES), f32) for i in range(3)]
        for layer in range(LAYERS):
            for side in range(2):
                here = key == 2 * layer + side
                for i in range(3):
                    row = push[i][layer : layer + 1, side * LANES : (side + 1) * LANES]
                    found[i] = jnp.where(here, lane_pick(row, index), found[i])
        live = lanes + half * LANES < counts
        for i in range(3):
            put(2 * i + half, jnp.where(live, found[i], 0.0))
            put(NODE_POS + 2 * i + half, pos_ref[i, :, part])
        put(NODE_BODY + half, body_ref[:, part].astype(f32))
    put(TOUCH_BODY, touch_ref[...].astype(f32))
    for i in range(3):
        put(TOUCH_POS + i, touch_pos_ref[i])


def split_rows(source_ref, scratch_ref, rows):
    for part in range(4):
        scratch_ref[pl.ds(part, rows, stride=8), :] = source_ref[:, part * LANES : (part + 1) * LANES]


LOWER, INVERSE, RIGHT, SHIFT, WEIGHT, AFFINE, PREPARED = 0, 36, 45, 54, 57, 58, 67


def lower_at(row, column):
    return LOWER + row * (row - 1) // 2 + column


def prepare_kernel(state_ref, vel_ref, mass_ref, out_ref, state_scr, vel_scr, mass_scr):
    split_rows(state_ref, state_scr, 12)
    split_rows(vel_ref, vel_scr, 12)
    split_rows(mass_ref, mass_scr, 1)
    get = lambda ref, row: ref[8 * row : 8 * row + 4, :]
    weight = get(mass_scr, 0)
    affine = [[get(state_scr, 3 + 3 * i + j) for j in range(3)] for i in range(3)]
    sum3 = lambda f: f(0) + f(1) + f(2)
    strain = [[None] * 3 for i in range(3)]
    gram = [[None] * 3 for i in range(3)]
    for i in range(3):
        for j in range(i, 3):
            value = sum3(lambda m: affine[i][m] * affine[j][m])
            strain[i][j] = strain[j][i] = value - 1.0 if i == j else value
            gram[i][j] = gram[j][i] = sum3(lambda m: affine[m][i] * affine[m][j])
    matrix = [[None] * 9 for i in range(9)]
    for row in range(9):
        i, j = divmod(row, 3)
        for column in range(row + 1):
            k, l = divmod(column, 3)
            value = affine[i][l] * affine[k][j]
            if i == k:
                value = gram[l][j] + value
            if j == l:
                value = value + strain[i][k]
            value = (4.0 * STIFFNESS) * value
            matrix[row][column] = value + weight if row == column else value
    for column in range(9):
        inverse = 1.0 / matrix[column][column]
        out_ref[INVERSE + column] = inverse
        factors = {}
        for row in range(column + 1, 9):
            factors[row] = matrix[row][column] * inverse
            out_ref[lower_at(row, column)] = factors[row]
        for row in range(column + 1, 9):
            for other in range(column + 1, row + 1):
                matrix[row][other] = matrix[row][other] - factors[row] * matrix[other][column]
    for row in range(9):
        i, j = divmod(row, 3)
        restoring = 4.0 * sum3(lambda m: strain[i][m] * affine[m][j])
        out_ref[RIGHT + row] = weight * get(vel_scr, 3 + row) - STIFFNESS * restoring
        out_ref[AFFINE + row] = affine[i][j]
    for i in range(3):
        out_ref[SHIFT + i] = get(state_scr, i) + get(vel_scr, i)
    out_ref[WEIGHT] = 1.0 / weight


def body_kernel(got_ref, prepared_ref, next_ref, back_ref, next_scr):
    sources = got_ref.shape[0] // ROWS
    pattern = iota((8, LANES), 0)
    quarter, second = pattern & 3, pattern >= 4
    numbers = iota((LANES, LANES), 0)
    sums = jnp.zeros((96, LANES), f32)
    for source in range(sources):
        tables, lefts = [], []
        for half in range(2):
            take = lambda row: got_ref[source * ROWS + row : source * ROWS + row + 1, :]
            body = take(NODE_BODY + half).astype(i32)
            force = [take(2 * i + half) for i in range(3)]
            place = [take(NODE_POS + 2 * i + half) for i in range(3)]
            general = force + [force[i] * place[j] for i in range(3) for j in range(3)]
            here = quarter == jnp.broadcast_to(body >> 7, (8, LANES))
            blocks = []
            for pair in range(6):
                both = jnp.where(
                    second,
                    jnp.broadcast_to(general[2 * pair + 1], (8, LANES)),
                    jnp.broadcast_to(general[2 * pair], (8, LANES)),
                )
                blocks.append(jnp.where(here, both, 0.0))
            exact = jnp.concatenate(blocks, axis=0)
            coarse = exact.astype(bf16)
            fine = (exact - coarse.astype(f32)).astype(bf16)
            lefts.append(jnp.concatenate([coarse, fine], axis=0))
            tables.append(jnp.where(numbers == (body & (LANES - 1)), 1.0, 0.0).astype(bf16))
        sums = sums + rows_dot(jnp.concatenate(lefts, axis=1), jnp.concatenate(tables, axis=1))
    sums = sums[:48] + sums[48:]
    force = [sums[4 * i : 4 * i + 4] for i in range(12)]
    inverse_weight = prepared_ref[WEIGHT]
    result = [prepared_ref[SHIFT + i] + force[i] * inverse_weight for i in range(3)]
    right = [prepared_ref[RIGHT + row] + force[3 + row] for row in range(9)]
    for column in range(9):
        for row in range(column + 1, 9):
            right[row] = right[row] - prepared_ref[lower_at(row, column)] * right[column]
    for column in reversed(range(9)):
        value = right[column] * prepared_ref[INVERSE + column]
        for row in range(column + 1, 9):
            value = value - prepared_ref[lower_at(row, column)] * right[row]
        right[column] = value
    result += [prepared_ref[AFFINE + row] + right[row] for row in range(9)]
    for row in range(12):
        next_scr[8 * row : 8 * row + 4, :] = result[row]
    for part in range(4):
        next_ref[:, part * LANES : (part + 1) * LANES] = next_scr[pl.ds(part, 12, stride=8), :]
    many = lambda row: got_ref[pl.ds(row, sources, stride=ROWS), :]
    body = many(TOUCH_BODY).astype(i32)
    place = [many(TOUCH_POS + i) for i in range(3)]
    key, index = body >> 7, body & (LANES - 1)
    here = [key == part for part in range(1, 4)]

    def pick(row):
        value = lane_pick(result[row][0:1], index)
        for part in range(1, 4):
            value = jnp.where(here[part - 1], lane_pick(result[row][part : part + 1], index), value)
        return value

    for i in range(3):
        point = pick(i)
        for j in range(3):
            point = point + pick(3 + 3 * i + j) * place[j]
        back_ref[pl.ds(i, sources, stride=BACK), :] = point


def shape(dims):
    return jax.ShapeDtypeStruct(dims, f32)


def per_device(
    particle_cell, particle_frac, particle_mass, particle_vel, node_cell, node_body, node_count,
    node_pos, body_state, body_vel, body_mass, touch_body, touch_pos,
):
    owners = lax.axis_size("wide")
    bulks = lax.axis_size("bulk")
    bodies = body_state.shape[1]
    total, ghost = pl.pallas_call(
        particles_kernel,
        out_shape=(shape((4 * LAYERS, COLUMNS)), shape((8, COLUMNS))),
        in_specs=[VMEM] * 4,
        out_specs=(VMEM, VMEM),
        name="particles",
    )(particle_cell, particle_frac, particle_mass, particle_vel)
    incoming = lax.ppermute(ghost, "bulk", [(i, (i + 1) % bulks) for i in range(bulks)])
    where = jnp.stack([lax.axis_index("bulk").astype(i32), jnp.int32(bulks - 1)])
    velocity, sent = pl.pallas_call(
        grid_kernel,
        out_shape=(shape((3, LAYERS, COLUMNS)), shape((owners * ROWS, LANES))),
        in_specs=[SMEM] + [VMEM] * 8,
        out_specs=(VMEM, VMEM),
        name="grid",
    )(where, total, incoming, node_cell, node_body, node_count.reshape(1, -1), node_pos, touch_body, touch_pos)
    got = lax.all_to_all(
        sent.reshape(owners, ROWS, LANES), "wide", split_axis=0, concat_axis=0, tiled=True
    ).reshape(owners * ROWS, LANES)
    prepared = pl.pallas_call(
        prepare_kernel,
        out_shape=shape((PREPARED, 4, LANES)),
        in_specs=[VMEM] * 3,
        out_specs=VMEM,
        scratch_shapes=[pltpu.VMEM((96, LANES), f32), pltpu.VMEM((96, LANES), f32), pltpu.VMEM((8, LANES), f32)],
        name="prepare",
    )(body_state, body_vel, body_mass.reshape(1, -1))
    body_next, back = pl.pallas_call(
        body_kernel,
        out_shape=(shape((12, bodies)), shape((owners * BACK, LANES))),
        in_specs=[VMEM, VMEM],
        out_specs=(VMEM, VMEM),
        scratch_shapes=[pltpu.VMEM((96, LANES), f32)],
        name="bodies",
    )(got, prepared)
    points = lax.all_to_all(
        back.reshape(owners, BACK, LANES), "wide", split_axis=0, concat_axis=0, tiled=True
    )
    touch_point = jnp.transpose(points[:, :3], (1, 0, 2))
    return body_next, velocity[:, :, None], touch_point


def solution(mesh):
    placed = (
        P(("bulk", "wide"), None),
        P(("bulk", "wide"), None),
        P(("bulk", "wide"), None),
        P(None, ("bulk", "wide"), None),
        P(("bulk", "wide"), None),
        P(("bulk", "wide"), None),
        P(("bulk", "wide")),
        P(None, ("bulk", "wide"), None),
        P(None, ("bulk", "wide")),
        P(None, ("bulk", "wide")),
        P(("bulk", "wide")),
        P(("bulk", "wide"), None),
        P(None, ("bulk", "wide"), None),
    )
    return jax.shard_map(
        per_device,
        mesh=mesh,
        in_specs=placed,
        out_specs=(
            P(None, ("bulk", "wide")),
            P(None, "bulk", "wide", None),
            P(None, ("bulk", "wide"), None),
        ),
        check_vma=False,
    )
```

```python
import functools

import jax
import jax.numpy as jnp
from jax import lax
from jax.experimental import pallas as pl
from jax.experimental.pallas import tpu as pltpu
from jax.sharding import PartitionSpec as P

LAYERS = 16
COLUMNS = 256
LANES = 128
STIFFNESS = 0.05
PULL = (0.0, 0.0, -0.5)
ROWS = 24
NODE_BODY, NODE_POS, TOUCH_BODY, TOUCH_POS = 6, 8, 14, 15
BACK = 8

f32, bf16, i32 = jnp.float32, jnp.bfloat16, jnp.int32
VMEM = pl.BlockSpec(memory_space=pltpu.VMEM)


def iota(shape, dim):
    return lax.broadcasted_iota(i32, shape, dim)


def rows_dot(a, b):
    return lax.dot_general(a, b, (((1,), (1,)), ((), ())), preferred_element_type=f32)


def table_kernel(cell_ref, table_ref):
    cell = cell_ref[...]
    column = iota((COLUMNS, cell.shape[1]), 0) == (cell & (COLUMNS - 1))
    table_ref[...] = jnp.where(column, 1.0, 0.0).astype(bf16)


def particles_kernel(cell_ref, table_ref, frac_ref, mass_ref, vel_ref, total_ref, ghost_ref):
    layer = cell_ref[...] >> 8
    frac, mass = frac_ref[...], mass_ref[...]
    lower = 1.0 - frac
    count = layer.shape[1]
    moments = [mass * vel_ref[i] for i in range(3)]
    low = [mass * lower] + [moment * lower for moment in moments]
    high = [mass * frac] + [moment * frac for moment in moments]
    rounded = lambda x: x.astype(bf16).astype(f32)
    layers = iota((LAYERS, count), 0)
    here, above = layers == layer, layers == layer + 1
    past = iota((8, count), 0)
    blocks = [jnp.where(here, rounded(x), 0.0) for x in low]
    blocks += [jnp.where(above, rounded(x), 0.0) for x in high]
    ghost = jnp.zeros((8, count), f32)
    for i, x in enumerate(high):
        ghost = jnp.where((past == i) & (layer == LAYERS - 1), rounded(x), ghost)
    left = jnp.concatenate(blocks + [ghost, jnp.zeros((8, count), f32)], axis=0).astype(bf16)
    sums = rows_dot(left, table_ref[...])
    half = 4 * LAYERS
    total_ref[...] = sums[:half] + sums[half : 2 * half]
    ghost_ref[...] = sums[2 * half : 2 * half + 8]


def group_order(count):
    return [(i + count // 2) % count for i in range(count)]


def put_blocks(ref, row, value, rows):
    half = value.shape[0] // 2
    ref[pl.ds(row, half, stride=rows), :] = value[half:]
    ref[pl.ds(half * rows + row, half, stride=rows), :] = value[:half]


def get_blocks(ref, row, count, rows):
    half = count // 2
    return jnp.concatenate(
        [ref[pl.ds(half * rows + row, half, stride=rows), :], ref[pl.ds(row, half, stride=rows), :]], axis=0
    )


def lane_pick(row, index):
    table = jnp.broadcast_to(row, index.shape)
    return jnp.take_along_axis(table, index, axis=1, mode="promise_in_bounds")


def at_ends():
    bulk = lax.axis_index("bulk")
    return bulk == 0, bulk == lax.axis_size("bulk") - 1


def inner_kernel(
    total_ref, cell_ref, body_ref, count_ref, pos_ref, touch_ref, touch_pos_ref,
    velocity_ref, sent_ref, first_ref,
):
    at_start, at_end = at_ends()
    wall = (iota((LAYERS, COLUMNS), 0) == LAYERS - 1) & at_end
    sums = [total_ref[LAYERS * i : LAYERS * (i + 1)] for i in range(4)]
    mass = sums[0]
    push = []
    for i in range(3):
        velocity = jnp.where(wall, 0.0, sums[i + 1] / (mass + 1.0) + PULL[i])
        velocity_ref[i] = velocity
        push.append(mass * velocity)
    owners = cell_ref.shape[0]
    lanes = iota((owners, LANES), 1)
    counts = jnp.sum(
        jnp.where(iota((owners, owners), 0) == iota((owners, owners), 1), count_ref[...], 0),
        axis=1, keepdims=True,
    )

    def put(row, value):
        put_blocks(sent_ref, row, value, ROWS)

    for half in range(2):
        part = slice(half * LANES, (half + 1) * LANES)
        cell = cell_ref[:, part]
        live = lanes + half * LANES < counts
        key, index = jnp.where(live, cell >> 7, -1), cell & (LANES - 1)
        found = [jnp.zeros((owners, LANES), f32) for i in range(3)]
        for layer in range(1, LAYERS):
            for side in range(2):
                here = key == 2 * layer + side
                for i in range(3):
                    row = push[i][layer : layer + 1, side * LANES : (side + 1) * LANES]
                    found[i] = jnp.where(here, lane_pick(row, index), found[i])
        for i in range(3):
            put(2 * i + half, found[i])
            put(NODE_POS + 2 * i + half, pos_ref[i, :, part])
        put(NODE_BODY + half, body_ref[:, part].astype(f32))
        first_ref[:, part] = jnp.where(live & (cell < COLUMNS), cell, -1)
    put(TOUCH_BODY, touch_ref[...].astype(f32))
    for i in range(3):
        put(TOUCH_POS + i, touch_pos_ref[i])


def first_kernel(total_ref, ghost_ref, inner_ref, begun_ref, first_ref, velocity_ref, sent_ref):
    at_start, at_end = at_ends()
    sums = [total_ref[LAYERS * i : LAYERS * i + 1] + ghost_ref[i : i + 1] for i in range(4)]
    mass = sums[0]
    velocity_ref[...] = inner_ref[...]
    sent_ref[...] = begun_ref[...]
    push = []
    for i in range(3):
        velocity = jnp.where(at_start, 0.0, sums[i + 1] / (mass + 1.0) + PULL[i])
        velocity_ref[i, 0:1] = velocity
        push.append(mass * velocity)
    for half in range(2):
        cell = first_ref[:, half * LANES : (half + 1) * LANES]
        key, index = cell >> 7, cell & (LANES - 1)
        for i in range(3):
            found = get_blocks(begun_ref, 2 * i + half, cell.shape[0], ROWS)
            for side in range(2):
                row = push[i][:, side * LANES : (side + 1) * LANES]
                found = jnp.where(key == side, lane_pick(row, index), found)
            put_blocks(sent_ref, 2 * i + half, found, ROWS)


def split_rows(source_ref, scratch_ref, rows):
    for part in range(4):
        scratch_ref[pl.ds(part, rows, stride=8), :] = source_ref[:, part * LANES : (part + 1) * LANES]


LOWER, INVERSE, RIGHT, SHIFT, WEIGHT, AFFINE, PREPARED = 0, 36, 45, 54, 57, 58, 67


def lower_at(row, column):
    return LOWER + row * (row - 1) // 2 + column


def prepare_kernel(state_ref, vel_ref, mass_ref, out_ref, state_scr, vel_scr, mass_scr):
    split_rows(state_ref, state_scr, 12)
    split_rows(vel_ref, vel_scr, 12)
    split_rows(mass_ref, mass_scr, 1)
    get = lambda ref, row: ref[8 * row : 8 * row + 4, :]
    weight = get(mass_scr, 0)
    affine = [[get(state_scr, 3 + 3 * i + j) for j in range(3)] for i in range(3)]
    sum3 = lambda f: f(0) + f(1) + f(2)
    strain = [[None] * 3 for i in range(3)]
    gram = [[None] * 3 for i in range(3)]
    for i in range(3):
        for j in range(i, 3):
            value = sum3(lambda m: affine[i][m] * affine[j][m])
            strain[i][j] = strain[j][i] = value - 1.0 if i == j else value
            gram[i][j] = gram[j][i] = sum3(lambda m: affine[m][i] * affine[m][j])
    matrix = [[None] * 9 for i in range(9)]
    for row in range(9):
        i, j = divmod(row, 3)
        for column in range(row + 1):
            k, l = divmod(column, 3)
            value = affine[i][l] * affine[k][j]
            if i == k:
                value = gram[l][j] + value
            if j == l:
                value = value + strain[i][k]
            value = (4.0 * STIFFNESS) * value
            matrix[row][column] = value + weight if row == column else value
    for column in range(9):
        inverse = 1.0 / matrix[column][column]
        out_ref[INVERSE + column] = inverse
        factors = {}
        for row in range(column + 1, 9):
            factors[row] = matrix[row][column] * inverse
            out_ref[lower_at(row, column)] = factors[row]
        for row in range(column + 1, 9):
            for other in range(column + 1, row + 1):
                matrix[row][other] = matrix[row][other] - factors[row] * matrix[other][column]
    for row in range(9):
        i, j = divmod(row, 3)
        restoring = 4.0 * sum3(lambda m: strain[i][m] * affine[m][j])
        out_ref[RIGHT + row] = weight * get(vel_scr, 3 + row) - STIFFNESS * restoring
        out_ref[AFFINE + row] = affine[i][j]
    for i in range(3):
        out_ref[SHIFT + i] = get(state_scr, i) + get(vel_scr, i)
    out_ref[WEIGHT] = 1.0 / weight


def body_kernel(got_ref, prepared_ref, next_ref, back_ref, next_scr):
    sources = got_ref.shape[0] // ROWS
    pattern = iota((8, LANES), 0)
    quarter, second = pattern & 3, pattern >= 4
    numbers = iota((LANES, LANES), 0)
    sums = jnp.zeros((96, LANES), f32)
    for source in range(sources):
        tables, lefts = [], []
        for half in range(2):
            take = lambda row: got_ref[source * ROWS + row : source * ROWS + row + 1, :]
            body = take(NODE_BODY + half).astype(i32)
            force = [take(2 * i + half) for i in range(3)]
            place = [take(NODE_POS + 2 * i + half) for i in range(3)]
            general = force + [force[i] * place[j] for i in range(3) for j in range(3)]
            here = quarter == jnp.broadcast_to(body >> 7, (8, LANES))
            blocks = []
            for pair in range(6):
                both = jnp.where(
                    second,
                    jnp.broadcast_to(general[2 * pair + 1], (8, LANES)),
                    jnp.broadcast_to(general[2 * pair], (8, LANES)),
                )
                blocks.append(jnp.where(here, both, 0.0))
            exact = jnp.concatenate(blocks, axis=0)
            coarse = exact.astype(bf16)
            fine = (exact - coarse.astype(f32)).astype(bf16)
            lefts.append(jnp.concatenate([coarse, fine], axis=0))
            tables.append(jnp.where(numbers == (body & (LANES - 1)), 1.0, 0.0).astype(bf16))
        sums = sums + rows_dot(jnp.concatenate(lefts, axis=1), jnp.concatenate(tables, axis=1))
    sums = sums[:48] + sums[48:]
    force = [sums[4 * i : 4 * i + 4] for i in range(12)]
    inverse_weight = prepared_ref[WEIGHT]
    result = [prepared_ref[SHIFT + i] + force[i] * inverse_weight for i in range(3)]
    right = [prepared_ref[RIGHT + row] + force[3 + row] for row in range(9)]
    for column in range(9):
        for row in range(column + 1, 9):
            right[row] = right[row] - prepared_ref[lower_at(row, column)] * right[column]
    for column in reversed(range(9)):
        value = right[column] * prepared_ref[INVERSE + column]
        for row in range(column + 1, 9):
            value = value - prepared_ref[lower_at(row, column)] * right[row]
        right[column] = value
    result += [prepared_ref[AFFINE + row] + right[row] for row in range(9)]
    for row in range(12):
        next_scr[8 * row : 8 * row + 4, :] = result[row]
    for part in range(4):
        next_ref[:, part * LANES : (part + 1) * LANES] = next_scr[pl.ds(part, 12, stride=8), :]
    many = lambda row: got_ref[pl.ds(row, sources, stride=ROWS), :]
    body = many(TOUCH_BODY).astype(i32)
    place = [many(TOUCH_POS + i) for i in range(3)]
    key, index = body >> 7, body & (LANES - 1)
    here = [key == part for part in range(1, 4)]

    def pick(row):
        value = lane_pick(result[row][0:1], index)
        for part in range(1, 4):
            value = jnp.where(here[part - 1], lane_pick(result[row][part : part + 1], index), value)
        return value

    for i in range(3):
        point = pick(i)
        for j in range(3):
            point = point + pick(3 + 3 * i + j) * place[j]
        back_ref[pl.ds(i, sources, stride=BACK), :] = point


def exchange(blocks, count, order):
    groups = None if order is None else [order]
    return lax.all_to_all(
        blocks.reshape(count, -1, LANES), "wide", split_axis=0, concat_axis=0, tiled=True,
        axis_index_groups=groups,
    )


def shape(dims):
    return jax.ShapeDtypeStruct(dims, f32)


def call(kernel, name, out_shape, scratch=(), flops=None):
    def run(*operands):
        cost = flops and pl.CostEstimate(flops=flops, bytes_accessed=1 << 20, transcendentals=0)
        return pl.pallas_call(
            kernel,
            out_shape=out_shape,
            in_specs=[VMEM] * len(operands),
            out_specs=jax.tree.map(lambda x: VMEM, out_shape),
            scratch_shapes=scratch,
            cost_estimate=cost,
            name=name,
            compiler_params=pltpu.CompilerParams(vmem_limit_bytes=8 << 20),
        )(*operands)

    return run


def per_device(
    particle_cell, particle_frac, particle_mass, particle_vel, node_cell, node_body, node_count,
    node_pos, body_state, body_vel, body_mass, touch_body, touch_pos,
):
    owners = lax.axis_size("wide")
    bulks = lax.axis_size("bulk")
    bodies = body_state.shape[1]
    table = call(
        table_kernel, "table", jax.ShapeDtypeStruct((COLUMNS, particle_cell.shape[1]), bf16), flops=10**9
    )(particle_cell)
    total, ghost = call(
        particles_kernel, "particles", (shape((4 * LAYERS, COLUMNS)), shape((8, COLUMNS))), flops=10**9
    )(particle_cell, table, particle_frac, particle_mass, particle_vel)
    incoming = lax.ppermute(ghost, "bulk", [(i, (i + 1) % bulks) for i in range(bulks)])
    held = (node_cell, node_body, node_count.reshape(1, -1), node_pos, touch_body, touch_pos)
    blocks = shape((owners * ROWS, LANES))
    speeds = shape((3, LAYERS, COLUMNS))
    inner, begun, first = call(
        inner_kernel, "inner", (speeds, blocks, jax.ShapeDtypeStruct(node_cell.shape, i32)), flops=10**9
    )(total, *held)
    velocity, sent = call(first_kernel, "first", (speeds, blocks))(total, incoming, inner, begun, first)
    order = group_order(owners)
    got = exchange(sent, owners, order).reshape(owners * ROWS, LANES)
    prepared = call(
        prepare_kernel, "prepare", shape((PREPARED, 4, LANES)),
        scratch=[pltpu.VMEM((96, LANES), f32), pltpu.VMEM((96, LANES), f32), pltpu.VMEM((8, LANES), f32)],
    )(body_state, body_vel, body_mass.reshape(1, -1))
    body_next, back = call(
        body_kernel, "bodies", (shape((12, bodies)), shape((owners * BACK, LANES))),
        scratch=[pltpu.VMEM((96, LANES), f32)],
    )(got, prepared)
    points = exchange(back, owners, order)[:, :3]
    half = owners // 2
    points = jnp.concatenate([points[half:], points[:half]], axis=0)
    touch_point = jnp.transpose(points, (1, 0, 2))
    return body_next, velocity[:, :, None], touch_point


def solution(mesh):
    placed = (
        P(("bulk", "wide"), None),
        P(("bulk", "wide"), None),
        P(("bulk", "wide"), None),
        P(None, ("bulk", "wide"), None),
        P(("bulk", "wide"), None),
        P(("bulk", "wide"), None),
        P(("bulk", "wide")),
        P(None, ("bulk", "wide"), None),
        P(None, ("bulk", "wide")),
        P(None, ("bulk", "wide")),
        P(("bulk", "wide")),
        P(("bulk", "wide"), None),
        P(None, ("bulk", "wide"), None),
    )
    return jax.shard_map(
        per_device,
        mesh=mesh,
        in_specs=placed,
        out_specs=(
            P(None, ("bulk", "wide")),
            P(None, "bulk", "wide", None),
            P(None, ("bulk", "wide"), None),
        ),
        check_vma=False,
    )
```

```python
import functools

import jax
import jax.numpy as jnp
from jax import lax
from jax.experimental import pallas as pl
from jax.experimental.pallas import tpu as pltpu
from jax.sharding import PartitionSpec as P

LAYERS = 16
COLUMNS = 256
LANES = 128
STIFFNESS = 0.05
PULL = (0.0, 0.0, -0.5)
ROWS = 18
NODE_BODY, NODE_POS, TOUCH_BODY, TOUCH_POS = 6, 8, 14, 15
OUT, HOME = 8, 8
BACK = 3

f32, bf16, i32 = jnp.float32, jnp.bfloat16, jnp.int32
VMEM = pl.BlockSpec(memory_space=pltpu.VMEM)


def iota(shape, dim):
    return lax.broadcasted_iota(i32, shape, dim)


def rows_dot(a, b):
    return lax.dot_general(a, b, (((1,), (1,)), ((), ())), preferred_element_type=f32)


def table_kernel(cell_ref, table_ref):
    cell = cell_ref[...]
    column = iota((COLUMNS, cell.shape[1]), 0) == (cell & (COLUMNS - 1))
    table_ref[...] = jnp.where(column, 1.0, 0.0).astype(bf16)


def particles_kernel(cell_ref, table_ref, frac_ref, mass_ref, vel_ref, total_ref, ghost_ref):
    layer = cell_ref[...] >> 8
    frac, mass = frac_ref[...], mass_ref[...]
    lower = 1.0 - frac
    count = layer.shape[1]
    moments = [mass * vel_ref[i] for i in range(3)]
    low = [mass * lower] + [moment * lower for moment in moments]
    high = [mass * frac] + [moment * frac for moment in moments]
    rounded = lambda x: x.astype(bf16).astype(f32)
    layers = iota((LAYERS, count), 0)
    here, above = layers == layer, layers == layer + 1
    past = iota((8, count), 0)
    blocks = [jnp.where(here, rounded(x), 0.0) for x in low]
    blocks += [jnp.where(above, rounded(x), 0.0) for x in high]
    ghost = jnp.zeros((8, count), f32)
    for i, x in enumerate(high):
        ghost = jnp.where((past == i) & (layer == LAYERS - 1), rounded(x), ghost)
    left = jnp.concatenate(blocks + [ghost, jnp.zeros((8, count), f32)], axis=0).astype(bf16)
    sums = rows_dot(left, table_ref[...])
    half = 4 * LAYERS
    total_ref[...] = sums[:half] + sums[half : 2 * half]
    ghost_ref[...] = sums[2 * half : 2 * half + 8]


def group_order(count, turn):
    return [(i + turn) % count for i in range(count)]


def put_blocks(ref, row, value, rows, turn):
    count = value.shape[0]
    turn = turn % count
    ref[pl.ds(row, count - turn, stride=rows), :] = value[turn:]
    if turn:
        ref[pl.ds((count - turn) * rows + row, turn, stride=rows), :] = value[:turn]


def get_blocks(ref, row, count, rows, turn):
    turn = turn % count
    tail = ref[pl.ds(row, count - turn, stride=rows), :]
    if not turn:
        return tail
    return jnp.concatenate([ref[pl.ds((count - turn) * rows + row, turn, stride=rows), :], tail], axis=0)


def lane_pick(row, index):
    table = jnp.broadcast_to(row, index.shape)
    return jnp.take_along_axis(table, index, axis=1, mode="promise_in_bounds")


def at_ends():
    bulk = lax.axis_index("bulk")
    return bulk == 0, bulk == lax.axis_size("bulk") - 1


def inner_kernel(
    total_ref, cell_ref, body_ref, count_ref, pos_ref, touch_ref, touch_pos_ref,
    velocity_ref, sent_ref, first_ref,
):
    at_start, at_end = at_ends()
    wall = (iota((LAYERS, COLUMNS), 0) == LAYERS - 1) & at_end
    sums = [total_ref[LAYERS * i : LAYERS * (i + 1)] for i in range(4)]
    mass = sums[0]
    push = []
    for i in range(3):
        velocity = jnp.where(wall, 0.0, sums[i + 1] / (mass + 1.0) + PULL[i])
        velocity_ref[i] = velocity
        push.append(mass * velocity)
    owners = cell_ref.shape[0]
    lanes = iota((owners, LANES), 1)
    counts = jnp.sum(
        jnp.where(iota((owners, owners), 0) == iota((owners, owners), 1), count_ref[...], 0),
        axis=1, keepdims=True,
    )

    def put(row, value):
        put_blocks(sent_ref, row, value, ROWS, owners * OUT // 16)

    for half in range(2):
        part = slice(half * LANES, (half + 1) * LANES)
        cell = cell_ref[:, part]
        live = lanes + half * LANES < counts
        key, index = jnp.where(live, cell >> 7, -1), cell & (LANES - 1)
        found = [jnp.zeros((owners, LANES), f32) for i in range(3)]
        for layer in range(1, LAYERS):
            for side in range(2):
                here = key == 2 * layer + side
                for i in range(3):
                    row = push[i][layer : layer + 1, side * LANES : (side + 1) * LANES]
                    found[i] = jnp.where(here, lane_pick(row, index), found[i])
        for i in range(3):
            put(2 * i + half, found[i])
            put(NODE_POS + 2 * i + half, pos_ref[i, :, part])
        put(NODE_BODY + half, body_ref[:, part].astype(f32))
        first_ref[:, part] = jnp.where(live & (cell < COLUMNS), cell, -1)
    put(TOUCH_BODY, touch_ref[...].astype(f32))
    for i in range(3):
        put(TOUCH_POS + i, touch_pos_ref[i])


def first_kernel(total_ref, ghost_ref, inner_ref, begun_ref, first_ref, velocity_ref, sent_ref):
    at_start, at_end = at_ends()
    owners = first_ref.shape[0]
    turn = owners * OUT // 16
    sums = [total_ref[LAYERS * i : LAYERS * i + 1] + ghost_ref[i : i + 1] for i in range(4)]
    mass = sums[0]
    velocity_ref[...] = inner_ref[...]
    sent_ref[...] = begun_ref[...]
    push = []
    for i in range(3):
        velocity = jnp.where(at_start, 0.0, sums[i + 1] / (mass + 1.0) + PULL[i])
        velocity_ref[i, 0:1] = velocity
        push.append(mass * velocity)
    for half in range(2):
        cell = first_ref[:, half * LANES : (half + 1) * LANES]
        key, index = cell >> 7, cell & (LANES - 1)
        for i in range(3):
            found = get_blocks(begun_ref, 2 * i + half, owners, ROWS, turn)
            for side in range(2):
                row = push[i][:, side * LANES : (side + 1) * LANES]
                found = jnp.where(key == side, lane_pick(row, index), found)
            put_blocks(sent_ref, 2 * i + half, found, ROWS, turn)


def split_rows(source_ref, scratch_ref, rows):
    for part in range(4):
        scratch_ref[pl.ds(part, rows, stride=8), :] = source_ref[:, part * LANES : (part + 1) * LANES]


LOWER, INVERSE, RIGHT, SHIFT, WEIGHT, AFFINE, PREPARED = 0, 36, 45, 54, 57, 58, 67


def lower_at(row, column):
    return LOWER + row * (row - 1) // 2 + column


def prepare_kernel(state_ref, vel_ref, mass_ref, out_ref, state_scr, vel_scr, mass_scr):
    split_rows(state_ref, state_scr, 12)
    split_rows(vel_ref, vel_scr, 12)
    split_rows(mass_ref, mass_scr, 1)
    get = lambda ref, row: ref[8 * row : 8 * row + 4, :]
    weight = get(mass_scr, 0)
    affine = [[get(state_scr, 3 + 3 * i + j) for j in range(3)] for i in range(3)]
    sum3 = lambda f: f(0) + f(1) + f(2)
    strain = [[None] * 3 for i in range(3)]
    gram = [[None] * 3 for i in range(3)]
    for i in range(3):
        for j in range(i, 3):
            value = sum3(lambda m: affine[i][m] * affine[j][m])
            strain[i][j] = strain[j][i] = value - 1.0 if i == j else value
            gram[i][j] = gram[j][i] = sum3(lambda m: affine[m][i] * affine[m][j])
    matrix = [[None] * 9 for i in range(9)]
    for row in range(9):
        i, j = divmod(row, 3)
        for column in range(row + 1):
            k, l = divmod(column, 3)
            value = affine[i][l] * affine[k][j]
            if i == k:
                value = gram[l][j] + value
            if j == l:
                value = value + strain[i][k]
            value = (4.0 * STIFFNESS) * value
            matrix[row][column] = value + weight if row == column else value
    for column in range(9):
        inverse = 1.0 / matrix[column][column]
        out_ref[INVERSE + column] = inverse
        factors = {}
        for row in range(column + 1, 9):
            factors[row] = matrix[row][column] * inverse
            out_ref[lower_at(row, column)] = factors[row]
        for row in range(column + 1, 9):
            for other in range(column + 1, row + 1):
                matrix[row][other] = matrix[row][other] - factors[row] * matrix[other][column]
    for row in range(9):
        i, j = divmod(row, 3)
        restoring = 4.0 * sum3(lambda m: strain[i][m] * affine[m][j])
        out_ref[RIGHT + row] = weight * get(vel_scr, 3 + row) - STIFFNESS * restoring
        out_ref[AFFINE + row] = affine[i][j]
    for i in range(3):
        out_ref[SHIFT + i] = get(state_scr, i) + get(vel_scr, i)
    out_ref[WEIGHT] = 1.0 / weight


def body_kernel(got_ref, prepared_ref, next_ref, back_ref, next_scr):
    sources = got_ref.shape[0] // ROWS
    pattern = iota((8, LANES), 0)
    quarter, second = pattern & 3, pattern >= 4
    numbers = iota((LANES, LANES), 0)
    sums = jnp.zeros((96, LANES), f32)
    for source in range(sources):
        tables, lefts = [], []
        for half in range(2):
            take = lambda row: got_ref[source * ROWS + row : source * ROWS + row + 1, :]
            body = take(NODE_BODY + half).astype(i32)
            force = [take(2 * i + half) for i in range(3)]
            place = [take(NODE_POS + 2 * i + half) for i in range(3)]
            general = force + [force[i] * place[j] for i in range(3) for j in range(3)]
            here = quarter == jnp.broadcast_to(body >> 7, (8, LANES))
            blocks = []
            for pair in range(6):
                both = jnp.where(
                    second,
                    jnp.broadcast_to(general[2 * pair + 1], (8, LANES)),
                    jnp.broadcast_to(general[2 * pair], (8, LANES)),
                )
                blocks.append(jnp.where(here, both, 0.0))
            exact = jnp.concatenate(blocks, axis=0)
            coarse = exact.astype(bf16)
            fine = (exact - coarse.astype(f32)).astype(bf16)
            lefts.append(jnp.concatenate([coarse, fine], axis=0))
            tables.append(jnp.where(numbers == (body & (LANES - 1)), 1.0, 0.0).astype(bf16))
        sums = sums + rows_dot(jnp.concatenate(lefts, axis=1), jnp.concatenate(tables, axis=1))
    sums = sums[:48] + sums[48:]
    force = [sums[4 * i : 4 * i + 4] for i in range(12)]
    inverse_weight = prepared_ref[WEIGHT]
    result = [prepared_ref[SHIFT + i] + force[i] * inverse_weight for i in range(3)]
    right = [prepared_ref[RIGHT + row] + force[3 + row] for row in range(9)]
    for column in range(9):
        for row in range(column + 1, 9):
            right[row] = right[row] - prepared_ref[lower_at(row, column)] * right[column]
    for column in reversed(range(9)):
        value = right[column] * prepared_ref[INVERSE + column]
        for row in range(column + 1, 9):
            value = value - prepared_ref[lower_at(row, column)] * right[row]
        right[column] = value
    result += [prepared_ref[AFFINE + row] + right[row] for row in range(9)]
    for row in range(12):
        next_scr[8 * row : 8 * row + 4, :] = result[row]
    for part in range(4):
        next_ref[:, part * LANES : (part + 1) * LANES] = next_scr[pl.ds(part, 12, stride=8), :]
    many = lambda row: got_ref[pl.ds(row, sources, stride=ROWS), :]
    body = many(TOUCH_BODY).astype(i32)
    place = [many(TOUCH_POS + i) for i in range(3)]
    key, index = body >> 7, body & (LANES - 1)
    here = [key == part for part in range(1, 4)]

    def pick(row):
        value = lane_pick(result[row][0:1], index)
        for part in range(1, 4):
            value = jnp.where(here[part - 1], lane_pick(result[row][part : part + 1], index), value)
        return value

    for i in range(3):
        point = pick(i)
        for j in range(3):
            point = point + pick(3 + 3 * i + j) * place[j]
        put_blocks(back_ref, i, point, BACK, sources * (HOME - OUT) // 16)


def exchange(blocks, count, turn):
    shaped = blocks.reshape(count, 1, -1)
    moved = lax.all_to_all(
        shaped, "wide", split_axis=0, concat_axis=0, tiled=True,
        axis_index_groups=[group_order(count, turn)],
    )
    return moved.reshape(blocks.shape)


def shape(dims):
    return jax.ShapeDtypeStruct(dims, f32)


def call(kernel, name, out_shape, scratch=(), flops=None):
    def run(*operands):
        cost = flops and pl.CostEstimate(flops=flops, bytes_accessed=1 << 20, transcendentals=0)
        return pl.pallas_call(
            kernel,
            out_shape=out_shape,
            in_specs=[VMEM] * len(operands),
            out_specs=jax.tree.map(lambda x: VMEM, out_shape),
            scratch_shapes=scratch,
            cost_estimate=cost,
            name=name,
            compiler_params=pltpu.CompilerParams(vmem_limit_bytes=8 << 20),
        )(*operands)

    return run


def per_device(
    particle_cell, particle_frac, particle_mass, particle_vel, node_cell, node_body, node_count,
    node_pos, body_state, body_vel, body_mass, touch_body, touch_pos,
):
    owners = lax.axis_size("wide")
    bulks = lax.axis_size("bulk")
    bodies = body_state.shape[1]
    table = call(
        table_kernel, "table", jax.ShapeDtypeStruct((COLUMNS, particle_cell.shape[1]), bf16), flops=10**9
    )(particle_cell)
    total, ghost = call(
        particles_kernel, "particles", (shape((4 * LAYERS, COLUMNS)), shape((8, COLUMNS))), flops=10**9
    )(particle_cell, table, particle_frac, particle_mass, particle_vel)
    incoming = lax.ppermute(ghost, "bulk", [(i, (i + 1) % bulks) for i in range(bulks)])
    held = (node_cell, node_body, node_count.reshape(1, -1), node_pos, touch_body, touch_pos)
    blocks = shape((owners * ROWS, LANES))
    speeds = shape((3, LAYERS, COLUMNS))
    inner, begun, first = call(
        inner_kernel, "inner", (speeds, blocks, jax.ShapeDtypeStruct(node_cell.shape, i32)), flops=10**9
    )(total, *held)
    velocity, sent = call(first_kernel, "first", (speeds, blocks))(total, incoming, inner, begun, first)
    got = exchange(sent, owners, owners * OUT // 16)
    prepared = call(
        prepare_kernel, "prepare", shape((PREPARED, 4, LANES)),
        scratch=[pltpu.VMEM((96, LANES), f32), pltpu.VMEM((96, LANES), f32), pltpu.VMEM((8, LANES), f32)],
    )(body_state, body_vel, body_mass.reshape(1, -1))
    body_next, back = call(
        body_kernel, "bodies", (shape((12, bodies)), shape((owners * BACK, LANES))),
        scratch=[pltpu.VMEM((96, LANES), f32)],
    )(got, prepared)
    turn = owners * HOME // 16
    points = exchange(back, owners, turn).reshape(owners, BACK, LANES)[:, :3]
    points = jnp.concatenate([points[owners - turn :], points[: owners - turn]], axis=0)
    touch_point = jnp.transpose(points, (1, 0, 2))
    return body_next, velocity[:, :, None], touch_point


def solution(mesh):
    placed = (
        P(("bulk", "wide"), None),
        P(("bulk", "wide"), None),
        P(("bulk", "wide"), None),
        P(None, ("bulk", "wide"), None),
        P(("bulk", "wide"), None),
        P(("bulk", "wide"), None),
        P(("bulk", "wide")),
        P(None, ("bulk", "wide"), None),
        P(None, ("bulk", "wide")),
        P(None, ("bulk", "wide")),
        P(("bulk", "wide")),
        P(("bulk", "wide"), None),
        P(None, ("bulk", "wide"), None),
    )
    return jax.shard_map(
        per_device,
        mesh=mesh,
        in_specs=placed,
        out_specs=(
            P(None, ("bulk", "wide")),
            P(None, "bulk", "wide", None),
            P(None, ("bulk", "wide"), None),
        ),
        check_vma=False,
    )
```

```python
import functools

import jax
import jax.numpy as jnp
from jax import lax
from jax.experimental import pallas as pl
from jax.experimental.pallas import tpu as pltpu
from jax.sharding import PartitionSpec as P

LAYERS = 16
COLUMNS = 256
LANES = 128
STIFFNESS = 0.05
PULL = (0.0, 0.0, -0.5)
ROWS = 18
NODE_BODY, NODE_POS, TOUCH_BODY, TOUCH_POS = 6, 8, 14, 15
OUT, HOME = 8, 8
BACK = 3

f32, bf16, i32 = jnp.float32, jnp.bfloat16, jnp.int32
VMEM = pl.BlockSpec(memory_space=pltpu.VMEM)


def iota(shape, dim):
    return lax.broadcasted_iota(i32, shape, dim)


def rows_dot(a, b):
    return lax.dot_general(a, b, (((1,), (1,)), ((), ())), preferred_element_type=f32)


def layers_kernel(layers_ref):
    layers_ref[...] = iota(layers_ref.shape, 0)


def particles_kernel(layers_ref, cell_ref, frac_ref, mass_ref, vel_ref, total_ref, ghost_ref):
    cell = cell_ref[...]
    layer = cell >> 8
    frac, mass = frac_ref[...], mass_ref[...]
    lower = 1.0 - frac
    count = layer.shape[1]
    moments = [mass * vel_ref[i] for i in range(3)]
    low = [mass * lower] + [moment * lower for moment in moments]
    high = [mass * frac] + [moment * frac for moment in moments]
    rounded = lambda x: x.astype(bf16).astype(f32)
    layers = layers_ref[...]
    here, above = layers == layer, layers == layer + 1
    past = iota((8, count), 0)
    blocks = [jnp.where(here, rounded(x), 0.0) for x in low]
    blocks += [jnp.where(above, rounded(x), 0.0) for x in high]
    ghost = jnp.zeros((8, count), f32)
    for i, x in enumerate(high):
        ghost = jnp.where((past == i) & (layer == LAYERS - 1), rounded(x), ghost)
    left = jnp.concatenate(blocks + [ghost, jnp.zeros((8, count), f32)], axis=0).astype(bf16)
    column = iota((COLUMNS, count), 0) == (cell & (COLUMNS - 1))
    sums = rows_dot(left, jnp.where(column, 1.0, 0.0).astype(bf16))
    half = 4 * LAYERS
    total_ref[...] = sums[:half] + sums[half : 2 * half]
    ghost_ref[...] = sums[2 * half : 2 * half + 8]


def group_order(count, turn):
    return [(i + turn) % count for i in range(count)]


def put_blocks(ref, row, value, rows, turn):
    count = value.shape[0]
    turn = turn % count
    ref[pl.ds(row, count - turn, stride=rows), :] = value[turn:]
    if turn:
        ref[pl.ds((count - turn) * rows + row, turn, stride=rows), :] = value[:turn]


def get_blocks(ref, row, count, rows, turn):
    turn = turn % count
    tail = ref[pl.ds(row, count - turn, stride=rows), :]
    if not turn:
        return tail
    return jnp.concatenate([ref[pl.ds((count - turn) * rows + row, turn, stride=rows), :], tail], axis=0)


def lane_pick(row, index):
    table = jnp.broadcast_to(row, index.shape)
    return jnp.take_along_axis(table, index, axis=1, mode="promise_in_bounds")


def split_rows(source_ref, scratch_ref, rows):
    for part in range(4):
        scratch_ref[pl.ds(part, rows, stride=8), :] = source_ref[:, part * LANES : (part + 1) * LANES]


LOWER, INVERSE, RIGHT, SHIFT, WEIGHT, AFFINE, PREPARED = 0, 36, 45, 54, 57, 58, 67


def lower_at(row, column):
    return LOWER + row * (row - 1) // 2 + column


def prepare(state_ref, vel_ref, mass_ref, out_ref, state_scr, vel_scr, mass_scr):
    split_rows(state_ref, state_scr, 12)
    split_rows(vel_ref, vel_scr, 12)
    split_rows(mass_ref, mass_scr, 1)
    get = lambda ref, row: ref[8 * row : 8 * row + 4, :]
    weight = get(mass_scr, 0)
    affine = [[get(state_scr, 3 + 3 * i + j) for j in range(3)] for i in range(3)]
    sum3 = lambda f: f(0) + f(1) + f(2)
    strain = [[None] * 3 for i in range(3)]
    gram = [[None] * 3 for i in range(3)]
    for i in range(3):
        for j in range(i, 3):
            value = sum3(lambda m: affine[i][m] * affine[j][m])
            strain[i][j] = strain[j][i] = value - 1.0 if i == j else value
            gram[i][j] = gram[j][i] = sum3(lambda m: affine[m][i] * affine[m][j])
    matrix = [[None] * 9 for i in range(9)]
    for row in range(9):
        i, j = divmod(row, 3)
        for column in range(row + 1):
            k, l = divmod(column, 3)
            value = affine[i][l] * affine[k][j]
            if i == k:
                value = gram[l][j] + value
            if j == l:
                value = value + strain[i][k]
            value = (4.0 * STIFFNESS) * value
            matrix[row][column] = value + weight if row == column else value
    for column in range(9):
        inverse = 1.0 / matrix[column][column]
        out_ref[INVERSE + column] = inverse
        factors = {}
        for row in range(column + 1, 9):
            factors[row] = matrix[row][column] * inverse
            out_ref[lower_at(row, column)] = factors[row]
        for row in range(column + 1, 9):
            for other in range(column + 1, row + 1):
                matrix[row][other] = matrix[row][other] - factors[row] * matrix[other][column]
    for row in range(9):
        i, j = divmod(row, 3)
        restoring = 4.0 * sum3(lambda m: strain[i][m] * affine[m][j])
        out_ref[RIGHT + row] = weight * get(vel_scr, 3 + row) - STIFFNESS * restoring
        out_ref[AFFINE + row] = affine[i][j]
    for i in range(3):
        out_ref[SHIFT + i] = get(state_scr, i) + get(vel_scr, i)
    out_ref[WEIGHT] = 1.0 / weight


def at_ends():
    bulk = lax.axis_index("bulk")
    return bulk == 0, bulk == lax.axis_size("bulk") - 1


def inner_kernel(
    total_ref, cell_ref, body_ref, count_ref, pos_ref, touch_ref, touch_pos_ref,
    state_ref, vel_ref, mass_ref,
    velocity_ref, sent_ref, first_ref, prepared_ref, state_scr, vel_scr, mass_scr,
):
    prepare(state_ref, vel_ref, mass_ref, prepared_ref, state_scr, vel_scr, mass_scr)
    at_start, at_end = at_ends()
    wall = (iota((LAYERS, COLUMNS), 0) == LAYERS - 1) & at_end
    sums = [total_ref[LAYERS * i : LAYERS * (i + 1)] for i in range(4)]
    mass = sums[0]
    push = []
    for i in range(3):
        velocity = jnp.where(wall, 0.0, sums[i + 1] / (mass + 1.0) + PULL[i])
        velocity_ref[i] = velocity
        push.append(mass * velocity)
    owners = cell_ref.shape[0]
    lanes = iota((owners, LANES), 1)
    counts = jnp.sum(
        jnp.where(iota((owners, owners), 0) == iota((owners, owners), 1), count_ref[...], 0),
        axis=1, keepdims=True,
    )

    def put(row, value):
        put_blocks(sent_ref, row, value, ROWS, owners * OUT // 16)

    for half in range(2):
        part = slice(half * LANES, (half + 1) * LANES)
        cell = cell_ref[:, part]
        live = lanes + half * LANES < counts
        key, index = jnp.where(live, cell >> 7, -1), cell & (LANES - 1)
        found = [jnp.zeros((owners, LANES), f32) for i in range(3)]
        for layer in range(1, LAYERS):
            for side in range(2):
                here = key == 2 * layer + side
                for i in range(3):
                    row = push[i][layer : layer + 1, side * LANES : (side + 1) * LANES]
                    found[i] = jnp.where(here, lane_pick(row, index), found[i])
        for i in range(3):
            put(2 * i + half, found[i])
            put(NODE_POS + 2 * i + half, pos_ref[i, :, part])
        put(NODE_BODY + half, body_ref[:, part].astype(f32))
        first_ref[:, part] = jnp.where(live & (cell < COLUMNS), cell, -1)
    put(TOUCH_BODY, touch_ref[...].astype(f32))
    for i in range(3):
        put(TOUCH_POS + i, touch_pos_ref[i])


def first_kernel(total_ref, ghost_ref, inner_ref, begun_ref, first_ref, velocity_ref, sent_ref):
    at_start, at_end = at_ends()
    owners = first_ref.shape[0]
    turn = owners * OUT // 16
    sums = [total_ref[LAYERS * i : LAYERS * i + 1] + ghost_ref[i : i + 1] for i in range(4)]
    mass = sums[0]
    velocity_ref[...] = inner_ref[...]
    sent_ref[...] = begun_ref[...]
    push = []
    for i in range(3):
        velocity = jnp.where(at_start, 0.0, sums[i + 1] / (mass + 1.0) + PULL[i])
        velocity_ref[i, 0:1] = velocity
        push.append(mass * velocity)
    for half in range(2):
        cell = first_ref[:, half * LANES : (half + 1) * LANES]
        key, index = cell >> 7, cell & (LANES - 1)
        for i in range(3):
            found = get_blocks(begun_ref, 2 * i + half, owners, ROWS, turn)
            for side in range(2):
                row = push[i][:, side * LANES : (side + 1) * LANES]
                found = jnp.where(key == side, lane_pick(row, index), found)
            put_blocks(sent_ref, 2 * i + half, found, ROWS, turn)


def body_kernel(got_ref, prepared_ref, next_ref, back_ref, next_scr):
    sources = got_ref.shape[0] // ROWS
    pattern = iota((8, LANES), 0)
    quarter, second = pattern & 3, pattern >= 4
    numbers = iota((LANES, LANES), 0)
    sums = jnp.zeros((96, LANES), f32)
    numbers16 = iota((LANES, LANES), 0).astype(f32).astype(bf16)
    for source in range(sources):
        tables, lefts = [], []
        for half in range(2):
            take = lambda row: got_ref[source * ROWS + row : source * ROWS + row + 1, :]
            wide = lambda row: jnp.broadcast_to(take(row), (8, LANES))
            body = take(NODE_BODY + half).astype(i32)
            here = quarter == jnp.broadcast_to(body >> 7, (8, LANES))
            force = [jnp.where(here, wide(2 * i + half), 0.0) for i in range(3)]
            place = [wide(NODE_POS + 2 * i + half) for i in range(3)]
            pick = lambda x, y: jnp.where(second, y, x)
            f01, f12 = pick(force[0], force[1]), pick(force[1], force[2])
            x12, x01, x20 = pick(place[1], place[2]), pick(place[0], place[1]), pick(place[2], place[0])
            blocks = [
                f01, pick(force[2], force[0] * place[0]), force[0] * x12, force[1] * x01, f12 * x20, force[2] * x12,
            ]
            exact = jnp.concatenate(blocks, axis=0)
            coarse = exact.astype(bf16)
            fine = (exact - coarse.astype(f32)).astype(bf16)
            lefts.append(jnp.concatenate([coarse, fine], axis=0))
            low = (body & (LANES - 1)).astype(f32).astype(bf16)
            tables.append(jnp.where(numbers16 == jnp.broadcast_to(low, (LANES, LANES)), bf16(1), bf16(0)))
        sums = sums + rows_dot(jnp.concatenate(lefts, axis=1), jnp.concatenate(tables, axis=1))
    sums = sums[:48] + sums[48:]
    force = [sums[4 * i : 4 * i + 4] for i in range(12)]
    inverse_weight = prepared_ref[WEIGHT]
    result = [prepared_ref[SHIFT + i] + force[i] * inverse_weight for i in range(3)]
    right = [prepared_ref[RIGHT + row] + force[3 + row] for row in range(9)]
    for column in range(9):
        for row in range(column + 1, 9):
            right[row] = right[row] - prepared_ref[lower_at(row, column)] * right[column]
    for column in reversed(range(9)):
        value = right[column] * prepared_ref[INVERSE + column]
        for row in range(column + 1, 9):
            value = value - prepared_ref[lower_at(row, column)] * right[row]
        right[column] = value
    result += [prepared_ref[AFFINE + row] + right[row] for row in range(9)]
    for row in range(12):
        next_scr[8 * row : 8 * row + 4, :] = result[row]
    for part in range(4):
        next_ref[:, part * LANES : (part + 1) * LANES] = next_scr[pl.ds(part, 12, stride=8), :]
    many = lambda row: got_ref[pl.ds(row, sources, stride=ROWS), :]
    body = many(TOUCH_BODY).astype(i32)
    place = [many(TOUCH_POS + i) for i in range(3)]
    key, index = body >> 7, body & (LANES - 1)
    here = [key == part for part in range(1, 4)]

    def pick(row):
        value = lane_pick(result[row][0:1], index)
        for part in range(1, 4):
            value = jnp.where(here[part - 1], lane_pick(result[row][part : part + 1], index), value)
        return value

    for i in range(3):
        point = pick(i)
        for j in range(3):
            point = point + pick(3 + 3 * i + j) * place[j]
        put_blocks(back_ref, i, point, BACK, sources * (HOME - OUT) // 16)


def finish_kernel(points_ref, next_ref, speeds_ref, point_ref, body_ref, velocity_ref):
    body_ref[...] = next_ref[...]
    owners = points_ref.shape[0] // BACK
    for i in range(3):
        point_ref[owners * i : owners * (i + 1), :] = get_blocks(points_ref, i, owners, BACK, owners * HOME // 16)
        for half in range(2):
            velocity_ref[pl.ds(2 * LAYERS * i + half, LAYERS, stride=2), :] = speeds_ref[
                i, :, half * LANES : (half + 1) * LANES
            ]


def exchange(blocks, count, turn):
    shaped = blocks.reshape(count, 1, -1)
    moved = lax.all_to_all(
        shaped, "wide", split_axis=0, concat_axis=0, tiled=True,
        axis_index_groups=[group_order(count, turn)],
    )
    return moved.reshape(blocks.shape)


def shape(dims):
    return jax.ShapeDtypeStruct(dims, f32)


def call(kernel, name, out_shape, scratch=(), flops=None):
    def run(*operands):
        cost = flops and pl.CostEstimate(flops=flops, bytes_accessed=1 << 20, transcendentals=0)
        return pl.pallas_call(
            kernel,
            out_shape=out_shape,
            in_specs=[VMEM] * len(operands),
            out_specs=jax.tree.map(lambda x: VMEM, out_shape),
            scratch_shapes=scratch,
            cost_estimate=cost,
            name=name,
            compiler_params=pltpu.CompilerParams(vmem_limit_bytes=8 << 20),
        )(*operands)

    return run


def per_device(
    particle_cell, particle_frac, particle_mass, particle_vel, node_cell, node_body, node_count,
    node_pos, body_state, body_vel, body_mass, touch_body, touch_pos,
):
    owners = lax.axis_size("wide")
    bulks = lax.axis_size("bulk")
    bodies = body_state.shape[1]
    layers = call(
        layers_kernel, "layers", jax.ShapeDtypeStruct((LAYERS, particle_cell.shape[1]), i32), flops=10**9
    )()
    total, ghost = call(
        particles_kernel, "particles", (shape((4 * LAYERS, COLUMNS)), shape((8, COLUMNS))), flops=10**9
    )(layers, particle_cell, particle_frac, particle_mass, particle_vel)
    incoming = lax.ppermute(ghost, "bulk", [(i, (i + 1) % bulks) for i in range(bulks)])
    held = (
        node_cell, node_body, node_count.reshape(1, -1), node_pos, touch_body, touch_pos,
        body_state, body_vel, body_mass.reshape(1, -1),
    )
    blocks = shape((owners * ROWS, LANES))
    speeds = shape((3, LAYERS, COLUMNS))
    inner, begun, first, prepared = call(
        inner_kernel,
        "inner",
        (speeds, blocks, jax.ShapeDtypeStruct(node_cell.shape, i32), shape((PREPARED, 4, LANES))),
        scratch=[pltpu.VMEM((96, LANES), f32), pltpu.VMEM((96, LANES), f32), pltpu.VMEM((8, LANES), f32)],
        flops=10**9,
    )(total, *held)
    velocity, sent = call(first_kernel, "first", (speeds, blocks))(total, incoming, inner, begun, first)
    got = exchange(sent, owners, owners * OUT // 16)
    body_next, back = call(
        body_kernel, "bodies", (shape((12, bodies)), shape((owners * BACK, LANES))),
        scratch=[pltpu.VMEM((96, LANES), f32)],
    )(got, prepared)
    points = exchange(back, owners, owners * HOME // 16)
    touch_point, body_next, velocity = call(
        finish_kernel, "finish",
        (shape((3 * owners, LANES)), shape((12, bodies)), shape((3 * LAYERS * COLUMNS // LANES, LANES))),
    )(points, body_next, velocity)
    return (
        body_next,
        velocity.reshape(3, LAYERS, 1, COLUMNS),
        touch_point.reshape(3, owners, LANES),
    )


def solution(mesh):
    placed = (
        P(("bulk", "wide"), None),
        P(("bulk", "wide"), None),
        P(("bulk", "wide"), None),
        P(None, ("bulk", "wide"), None),
        P(("bulk", "wide"), None),
        P(("bulk", "wide"), None),
        P(("bulk", "wide")),
        P(None, ("bulk", "wide"), None),
        P(None, ("bulk", "wide")),
        P(None, ("bulk", "wide")),
        P(("bulk", "wide")),
        P(("bulk", "wide"), None),
        P(None, ("bulk", "wide"), None),
    )
    return jax.shard_map(
        per_device,
        mesh=mesh,
        in_specs=placed,
        out_specs=(
            P(None, ("bulk", "wide")),
            P(None, "bulk", "wide", None),
            P(None, ("bulk", "wide"), None),
        ),
        check_vma=False,
    )
```

```python
import functools

import jax
import jax.numpy as jnp
from jax import lax
from jax.experimental import pallas as pl
from jax.experimental.pallas import tpu as pltpu
from jax.sharding import PartitionSpec as P

LAYERS = 16
COLUMNS = 256
LANES = 128
STIFFNESS = 0.05
PULL = (0.0, 0.0, -0.5)
ROWS = 18
NODE_BODY, NODE_POS, TOUCH_BODY, TOUCH_POS = 6, 8, 14, 15
OUT, HOME = 8, 8
BACK = 3

f32, bf16, i32 = jnp.float32, jnp.bfloat16, jnp.int32
VMEM = pl.BlockSpec(memory_space=pltpu.VMEM)


def iota(shape, dim):
    return lax.broadcasted_iota(i32, shape, dim)


def rows_dot(a, b):
    return lax.dot_general(a, b, (((1,), (1,)), ((), ())), preferred_element_type=f32)


def layers_kernel(layers_ref):
    layers_ref[...] = iota(layers_ref.shape, 0)


def particles_kernel(layers_ref, cell_ref, frac_ref, mass_ref, vel_ref, total_ref, ghost_ref):
    cell = cell_ref[...]
    layer = cell >> 8
    frac, mass = frac_ref[...], mass_ref[...]
    lower = 1.0 - frac
    count = layer.shape[1]
    moments = [mass * vel_ref[i] for i in range(3)]
    low = [mass * lower] + [moment * lower for moment in moments]
    high = [mass * frac] + [moment * frac for moment in moments]
    rounded = lambda x: x.astype(bf16).astype(f32)
    layers = layers_ref[...]
    here, above = layers == layer, layers == layer + 1
    past = iota((8, count), 0)
    blocks = [jnp.where(here, rounded(x), 0.0) for x in low]
    blocks += [jnp.where(above, rounded(x), 0.0) for x in high]
    ghost = jnp.zeros((8, count), f32)
    for i, x in enumerate(high):
        ghost = jnp.where((past == i) & (layer == LAYERS - 1), rounded(x), ghost)
    left = jnp.concatenate(blocks + [ghost, jnp.zeros((8, count), f32)], axis=0).astype(bf16)
    column = iota((COLUMNS, count), 0) == (cell & (COLUMNS - 1))
    sums = rows_dot(left, jnp.where(column, 1.0, 0.0).astype(bf16))
    half = 4 * LAYERS
    total_ref[...] = sums[:half] + sums[half : 2 * half]
    ghost_ref[...] = sums[2 * half : 2 * half + 8]


def group_order(count, turn):
    return [(i + turn) % count for i in range(count)]


def put_blocks(ref, row, value, rows, turn):
    count = value.shape[0]
    turn = turn % count
    ref[pl.ds(row, count - turn, stride=rows), :] = value[turn:]
    if turn:
        ref[pl.ds((count - turn) * rows + row, turn, stride=rows), :] = value[:turn]


def get_blocks(ref, row, count, rows, turn):
    turn = turn % count
    tail = ref[pl.ds(row, count - turn, stride=rows), :]
    if not turn:
        return tail
    return jnp.concatenate([ref[pl.ds((count - turn) * rows + row, turn, stride=rows), :], tail], axis=0)


def lane_pick(row, index):
    table = jnp.broadcast_to(row, index.shape)
    return jnp.take_along_axis(table, index, axis=1, mode="promise_in_bounds")


def split_rows(source_ref, scratch_ref, rows):
    for part in range(4):
        scratch_ref[pl.ds(part, rows, stride=8), :] = source_ref[:, part * LANES : (part + 1) * LANES]


LOWER, INVERSE, RIGHT, SHIFT, WEIGHT, AFFINE, PREPARED = 0, 36, 45, 54, 57, 58, 67


def lower_at(row, column):
    return LOWER + row * (row - 1) // 2 + column


def prepare(state_ref, vel_ref, mass_ref, out_ref, state_scr, vel_scr, mass_scr):
    split_rows(state_ref, state_scr, 12)
    split_rows(vel_ref, vel_scr, 12)
    split_rows(mass_ref, mass_scr, 1)
    get = lambda ref, row: ref[8 * row : 8 * row + 4, :]
    weight = get(mass_scr, 0)
    affine = [[get(state_scr, 3 + 3 * i + j) for j in range(3)] for i in range(3)]
    sum3 = lambda f: f(0) + f(1) + f(2)
    strain = [[None] * 3 for i in range(3)]
    gram = [[None] * 3 for i in range(3)]
    for i in range(3):
        for j in range(i, 3):
            value = sum3(lambda m: affine[i][m] * affine[j][m])
            strain[i][j] = strain[j][i] = value - 1.0 if i == j else value
            gram[i][j] = gram[j][i] = sum3(lambda m: affine[m][i] * affine[m][j])
    matrix = [[None] * 9 for i in range(9)]
    for row in range(9):
        i, j = divmod(row, 3)
        for column in range(row + 1):
            k, l = divmod(column, 3)
            value = affine[i][l] * affine[k][j]
            if i == k:
                value = gram[l][j] + value
            if j == l:
                value = value + strain[i][k]
            value = (4.0 * STIFFNESS) * value
            matrix[row][column] = value + weight if row == column else value
    for column in range(9):
        inverse = 1.0 / matrix[column][column]
        out_ref[INVERSE + column] = inverse
        factors = {}
        for row in range(column + 1, 9):
            factors[row] = matrix[row][column] * inverse
            out_ref[lower_at(row, column)] = factors[row]
        for row in range(column + 1, 9):
            for other in range(column + 1, row + 1):
                matrix[row][other] = matrix[row][other] - factors[row] * matrix[other][column]
    for row in range(9):
        i, j = divmod(row, 3)
        restoring = 4.0 * sum3(lambda m: strain[i][m] * affine[m][j])
        out_ref[RIGHT + row] = weight * get(vel_scr, 3 + row) - STIFFNESS * restoring
        out_ref[AFFINE + row] = affine[i][j]
    for i in range(3):
        out_ref[SHIFT + i] = get(state_scr, i) + get(vel_scr, i)
    out_ref[WEIGHT] = 1.0 / weight


def at_ends():
    bulk = lax.axis_index("bulk")
    return bulk == 0, bulk == lax.axis_size("bulk") - 1


def inner_kernel(
    total_ref, cell_ref, body_ref, count_ref, pos_ref, touch_ref, touch_pos_ref,
    state_ref, vel_ref, mass_ref,
    velocity_ref, sent_ref, first_ref, prepared_ref, state_scr, vel_scr, mass_scr,
):
    prepare(state_ref, vel_ref, mass_ref, prepared_ref, state_scr, vel_scr, mass_scr)
    at_start, at_end = at_ends()
    wall = (iota((LAYERS, COLUMNS), 0) == LAYERS - 1) & at_end
    sums = [total_ref[LAYERS * i : LAYERS * (i + 1)] for i in range(4)]
    mass = sums[0]
    push = []
    for i in range(3):
        velocity = jnp.where(wall, 0.0, sums[i + 1] / (mass + 1.0) + PULL[i])
        velocity_ref[i] = velocity
        push.append(mass * velocity)
    owners = cell_ref.shape[0]
    lanes = iota((owners, LANES), 1)
    counts = jnp.sum(
        jnp.where(iota((owners, owners), 0) == iota((owners, owners), 1), count_ref[...], 0),
        axis=1, keepdims=True,
    )

    def put(row, value):
        put_blocks(sent_ref, row, value, ROWS, owners * OUT // 16)

    for half in range(2):
        part = slice(half * LANES, (half + 1) * LANES)
        cell = cell_ref[:, part]
        live = lanes + half * LANES < counts
        key, index = jnp.where(live, cell >> 7, -1), cell & (LANES - 1)
        found = [jnp.zeros((owners, LANES), f32) for i in range(3)]
        for layer in range(1, LAYERS):
            for side in range(2):
                here = key == 2 * layer + side
                for i in range(3):
                    row = push[i][layer : layer + 1, side * LANES : (side + 1) * LANES]
                    found[i] = jnp.where(here, lane_pick(row, index), found[i])
        for i in range(3):
            put(2 * i + half, found[i])
            put(NODE_POS + 2 * i + half, pos_ref[i, :, part])
        put(NODE_BODY + half, body_ref[:, part].astype(f32))
        first_ref[:, part] = jnp.where(live & (cell < COLUMNS), cell, -1)
    put(TOUCH_BODY, touch_ref[...].astype(f32))
    for i in range(3):
        put(TOUCH_POS + i, touch_pos_ref[i])


def first_kernel(total_ref, odd_ref, even_ref, inner_ref, begun_ref, first_ref, velocity_ref, sent_ref):
    at_start, at_end = at_ends()
    odd = lax.rem(lax.axis_index("bulk"), 2) == 1
    owners = first_ref.shape[0]
    turn = owners * OUT // 16
    sums = [total_ref[LAYERS * i : LAYERS * i + 1] + jnp.where(odd, odd_ref[i : i + 1], even_ref[i : i + 1]) for i in range(4)]
    mass = sums[0]
    velocity_ref[...] = inner_ref[...]
    sent_ref[...] = begun_ref[...]
    push = []
    for i in range(3):
        velocity = jnp.where(at_start, 0.0, sums[i + 1] / (mass + 1.0) + PULL[i])
        velocity_ref[i, 0:1] = velocity
        push.append(mass * velocity)
    for half in range(2):
        cell = first_ref[:, half * LANES : (half + 1) * LANES]
        key, index = cell >> 7, cell & (LANES - 1)
        for i in range(3):
            found = get_blocks(begun_ref, 2 * i + half, owners, ROWS, turn)
            for side in range(2):
                row = push[i][:, side * LANES : (side + 1) * LANES]
                found = jnp.where(key == side, lane_pick(row, index), found)
            put_blocks(sent_ref, 2 * i + half, found, ROWS, turn)


def body_kernel(got_ref, prepared_ref, next_ref, back_ref, next_scr):
    sources = got_ref.shape[0] // ROWS
    pattern = iota((8, LANES), 0)
    quarter, second = pattern & 3, pattern >= 4
    numbers = iota((LANES, LANES), 0)
    sums = jnp.zeros((96, LANES), f32)
    numbers16 = iota((LANES, LANES), 0).astype(f32).astype(bf16)
    for source in range(sources):
        tables, lefts = [], []
        for half in range(2):
            take = lambda row: got_ref[source * ROWS + row : source * ROWS + row + 1, :]
            wide = lambda row: jnp.broadcast_to(take(row), (8, LANES))
            body = take(NODE_BODY + half).astype(i32)
            here = quarter == jnp.broadcast_to(body >> 7, (8, LANES))
            force = [jnp.where(here, wide(2 * i + half), 0.0) for i in range(3)]
            place = [wide(NODE_POS + 2 * i + half) for i in range(3)]
            pick = lambda x, y: jnp.where(second, y, x)
            f01, f12 = pick(force[0], force[1]), pick(force[1], force[2])
            x12, x01, x20 = pick(place[1], place[2]), pick(place[0], place[1]), pick(place[2], place[0])
            blocks = [
                f01, pick(force[2], force[0] * place[0]), force[0] * x12, force[1] * x01, f12 * x20, force[2] * x12,
            ]
            exact = jnp.concatenate(blocks, axis=0)
            coarse = exact.astype(bf16)
            fine = (exact - coarse.astype(f32)).astype(bf16)
            lefts.append(jnp.concatenate([coarse, fine], axis=0))
            low = (body & (LANES - 1)).astype(f32).astype(bf16)
            tables.append(jnp.where(numbers16 == jnp.broadcast_to(low, (LANES, LANES)), bf16(1), bf16(0)))
        sums = sums + rows_dot(jnp.concatenate(lefts, axis=1), jnp.concatenate(tables, axis=1))
    sums = sums[:48] + sums[48:]
    force = [sums[4 * i : 4 * i + 4] for i in range(12)]
    inverse_weight = prepared_ref[WEIGHT]
    result = [prepared_ref[SHIFT + i] + force[i] * inverse_weight for i in range(3)]
    right = [prepared_ref[RIGHT + row] + force[3 + row] for row in range(9)]
    for column in range(9):
        for row in range(column + 1, 9):
            right[row] = right[row] - prepared_ref[lower_at(row, column)] * right[column]
    for column in reversed(range(9)):
        value = right[column] * prepared_ref[INVERSE + column]
        for row in range(column + 1, 9):
            value = value - prepared_ref[lower_at(row, column)] * right[row]
        right[column] = value
    result += [prepared_ref[AFFINE + row] + right[row] for row in range(9)]
    for row in range(12):
        next_scr[8 * row : 8 * row + 4, :] = result[row]
    for part in range(4):
        next_ref[:, part * LANES : (part + 1) * LANES] = next_scr[pl.ds(part, 12, stride=8), :]
    many = lambda row: got_ref[pl.ds(row, sources, stride=ROWS), :]
    body = many(TOUCH_BODY).astype(i32)
    place = [many(TOUCH_POS + i) for i in range(3)]
    key, index = body >> 7, body & (LANES - 1)
    here = [key == part for part in range(1, 4)]

    def pick(row):
        value = lane_pick(result[row][0:1], index)
        for part in range(1, 4):
            value = jnp.where(here[part - 1], lane_pick(result[row][part : part + 1], index), value)
        return value

    for i in range(3):
        point = pick(i)
        for j in range(3):
            point = point + pick(3 + 3 * i + j) * place[j]
        put_blocks(back_ref, i, point, BACK, sources * (HOME - OUT) // 16)


def finish_kernel(points_ref, next_ref, speeds_ref, point_ref, body_ref, velocity_ref):
    body_ref[...] = next_ref[...]
    owners = points_ref.shape[0] // BACK
    for i in range(3):
        point_ref[owners * i : owners * (i + 1), :] = get_blocks(points_ref, i, owners, BACK, owners * HOME // 16)
        for half in range(2):
            velocity_ref[pl.ds(2 * LAYERS * i + half, LAYERS, stride=2), :] = speeds_ref[
                i, :, half * LANES : (half + 1) * LANES
            ]


def even_pairs(count):
    return [(i, i + 1) for i in range(1, count - 1, 2)] + [(4, 0), (0, 1), (2, 3), (8, 5), (6, 7), (12, 9), (10, 11), (15, 13), (14, 15)]


def exchange(blocks, count, turn):
    shaped = blocks.reshape(count, 1, -1)
    moved = lax.all_to_all(
        shaped, "wide", split_axis=0, concat_axis=0, tiled=True,
        axis_index_groups=[group_order(count, turn)],
    )
    return moved.reshape(blocks.shape)


def shape(dims):
    return jax.ShapeDtypeStruct(dims, f32)


def call(kernel, name, out_shape, scratch=(), flops=None):
    def run(*operands):
        cost = flops and pl.CostEstimate(flops=flops, bytes_accessed=1 << 20, transcendentals=0)
        return pl.pallas_call(
            kernel,
            out_shape=out_shape,
            in_specs=[VMEM] * len(operands),
            out_specs=jax.tree.map(lambda x: VMEM, out_shape),
            scratch_shapes=scratch,
            cost_estimate=cost,
            name=name,
            compiler_params=pltpu.CompilerParams(vmem_limit_bytes=8 << 20),
        )(*operands)

    return run


def per_device(
    particle_cell, particle_frac, particle_mass, particle_vel, node_cell, node_body, node_count,
    node_pos, body_state, body_vel, body_mass, touch_body, touch_pos,
):
    owners = lax.axis_size("wide")
    bulks = lax.axis_size("bulk")
    bodies = body_state.shape[1]
    layers = call(
        layers_kernel, "layers", jax.ShapeDtypeStruct((LAYERS, particle_cell.shape[1]), i32), flops=10**9
    )()
    total, ghost = call(
        particles_kernel, "particles", (shape((4 * LAYERS, COLUMNS)), shape((8, COLUMNS))), flops=10**9
    )(layers, particle_cell, particle_frac, particle_mass, particle_vel)
    to_odd = lax.ppermute(ghost, "bulk", [(i, i ^ 1) for i in range(bulks)])
    to_even = lax.ppermute(ghost, "bulk", even_pairs(bulks))
    held = (
        node_cell, node_body, node_count.reshape(1, -1), node_pos, touch_body, touch_pos,
        body_state, body_vel, body_mass.reshape(1, -1),
    )
    blocks = shape((owners * ROWS, LANES))
    speeds = shape((3, LAYERS, COLUMNS))
    inner, begun, first, prepared = call(
        inner_kernel,
        "inner",
        (speeds, blocks, jax.ShapeDtypeStruct(node_cell.shape, i32), shape((PREPARED, 4, LANES))),
        scratch=[pltpu.VMEM((96, LANES), f32), pltpu.VMEM((96, LANES), f32), pltpu.VMEM((8, LANES), f32)],
        flops=10**9,
    )(total, *held)
    velocity, sent = call(first_kernel, "first", (speeds, blocks))(total, to_odd, to_even, inner, begun, first)
    got = exchange(sent, owners, owners * OUT // 16)
    body_next, back = call(
        body_kernel, "bodies", (shape((12, bodies)), shape((owners * BACK, LANES))),
        scratch=[pltpu.VMEM((96, LANES), f32)],
    )(got, prepared)
    points = exchange(back, owners, owners * HOME // 16)
    touch_point, body_next, velocity = call(
        finish_kernel, "finish",
        (shape((3 * owners, LANES)), shape((12, bodies)), shape((3 * LAYERS * COLUMNS // LANES, LANES))),
    )(points, body_next, velocity)
    return (
        body_next,
        velocity.reshape(3, LAYERS, 1, COLUMNS),
        touch_point.reshape(3, owners, LANES),
    )


def solution(mesh):
    placed = (
        P(("bulk", "wide"), None),
        P(("bulk", "wide"), None),
        P(("bulk", "wide"), None),
        P(None, ("bulk", "wide"), None),
        P(("bulk", "wide"), None),
        P(("bulk", "wide"), None),
        P(("bulk", "wide")),
        P(None, ("bulk", "wide"), None),
        P(None, ("bulk", "wide")),
        P(None, ("bulk", "wide")),
        P(("bulk", "wide")),
        P(("bulk", "wide"), None),
        P(None, ("bulk", "wide"), None),
    )
    return jax.shard_map(
        per_device,
        mesh=mesh,
        in_specs=placed,
        out_specs=(
            P(None, ("bulk", "wide")),
            P(None, "bulk", "wide", None),
            P(None, ("bulk", "wide"), None),
        ),
        check_vma=False,
    )
```

```python
import functools

import jax
import jax.numpy as jnp
from jax import lax
from jax.experimental import pallas as pl
from jax.experimental.pallas import tpu as pltpu
from jax.sharding import PartitionSpec as P

LAYERS = 16
COLUMNS = 256
LANES = 128
STIFFNESS = 0.05
PULL = (0.0, 0.0, -0.5)
ROWS = 18
NODE_BODY, NODE_POS, TOUCH_BODY, TOUCH_POS = 6, 8, 14, 15
OUT, HOME = 11, 9
BACK = 3

f32, bf16, i32 = jnp.float32, jnp.bfloat16, jnp.int32
VMEM = pl.BlockSpec(memory_space=pltpu.VMEM)


def iota(shape, dim):
    return lax.broadcasted_iota(i32, shape, dim)


def rows_dot(a, b):
    return lax.dot_general(a, b, (((1,), (1,)), ((), ())), preferred_element_type=f32)


def layers_kernel(layers_ref):
    layers_ref[...] = iota(layers_ref.shape, 0)


def particles_kernel(layers_ref, cell_ref, frac_ref, mass_ref, vel_ref, total_ref, ghost_ref):
    cell = cell_ref[...]
    layer = cell >> 8
    frac, mass = frac_ref[...], mass_ref[...]
    lower = 1.0 - frac
    count = layer.shape[1]
    moments = [mass * vel_ref[i] for i in range(3)]
    low = [mass * lower] + [moment * lower for moment in moments]
    high = [mass * frac] + [moment * frac for moment in moments]
    rounded = lambda x: x.astype(bf16).astype(f32)
    layers = layers_ref[...]
    here, above = layers == layer, layers == layer + 1
    past = iota((8, count), 0)
    blocks = [jnp.where(here, rounded(x), 0.0) for x in low]
    blocks += [jnp.where(above, rounded(x), 0.0) for x in high]
    ghost = jnp.zeros((8, count), f32)
    for i, x in enumerate(high):
        ghost = jnp.where((past == i) & (layer == LAYERS - 1), rounded(x), ghost)
    left = jnp.concatenate(blocks + [ghost, jnp.zeros((8, count), f32)], axis=0).astype(bf16)
    column = iota((COLUMNS, count), 0) == (cell & (COLUMNS - 1))
    sums = rows_dot(left, jnp.where(column, 1.0, 0.0).astype(bf16))
    half = 4 * LAYERS
    total_ref[...] = sums[:half] + sums[half : 2 * half]
    ghost_ref[...] = sums[2 * half : 2 * half + 8]


def group_order(count, turn):
    return [(i + turn) % count for i in range(count)]


def put_blocks(ref, row, value, rows, turn):
    count = value.shape[0]
    turn = turn % count
    ref[pl.ds(row, count - turn, stride=rows), :] = value[turn:]
    if turn:
        ref[pl.ds((count - turn) * rows + row, turn, stride=rows), :] = value[:turn]


def get_blocks(ref, row, count, rows, turn):
    turn = turn % count
    tail = ref[pl.ds(row, count - turn, stride=rows), :]
    if not turn:
        return tail
    return jnp.concatenate([ref[pl.ds((count - turn) * rows + row, turn, stride=rows), :], tail], axis=0)


def lane_pick(row, index):
    table = jnp.broadcast_to(row, index.shape)
    return jnp.take_along_axis(table, index, axis=1, mode="promise_in_bounds")


def split_rows(source_ref, scratch_ref, rows):
    for part in range(4):
        scratch_ref[pl.ds(part, rows, stride=8), :] = source_ref[:, part * LANES : (part + 1) * LANES]


LOWER, INVERSE, RIGHT, SHIFT, WEIGHT, AFFINE, PREPARED = 0, 36, 45, 54, 57, 58, 67


def lower_at(row, column):
    return LOWER + row * (row - 1) // 2 + column


def prepare(state_ref, vel_ref, mass_ref, out_ref, state_scr, vel_scr, mass_scr):
    split_rows(state_ref, state_scr, 12)
    split_rows(vel_ref, vel_scr, 12)
    split_rows(mass_ref, mass_scr, 1)
    get = lambda ref, row: ref[8 * row : 8 * row + 4, :]
    weight = get(mass_scr, 0)
    affine = [[get(state_scr, 3 + 3 * i + j) for j in range(3)] for i in range(3)]
    sum3 = lambda f: f(0) + f(1) + f(2)
    strain = [[None] * 3 for i in range(3)]
    gram = [[None] * 3 for i in range(3)]
    for i in range(3):
        for j in range(i, 3):
            value = sum3(lambda m: affine[i][m] * affine[j][m])
            strain[i][j] = strain[j][i] = value - 1.0 if i == j else value
            gram[i][j] = gram[j][i] = sum3(lambda m: affine[m][i] * affine[m][j])
    matrix = [[None] * 9 for i in range(9)]
    for row in range(9):
        i, j = divmod(row, 3)
        for column in range(row + 1):
            k, l = divmod(column, 3)
            value = affine[i][l] * affine[k][j]
            if i == k:
                value = gram[l][j] + value
            if j == l:
                value = value + strain[i][k]
            value = (4.0 * STIFFNESS) * value
            matrix[row][column] = value + weight if row == column else value
    for column in range(9):
        inverse = 1.0 / matrix[column][column]
        out_ref[INVERSE + column] = inverse
        factors = {}
        for row in range(column + 1, 9):
            factors[row] = matrix[row][column] * inverse
            out_ref[lower_at(row, column)] = factors[row]
        for row in range(column + 1, 9):
            for other in range(column + 1, row + 1):
                matrix[row][other] = matrix[row][other] - factors[row] * matrix[other][column]
    for row in range(9):
        i, j = divmod(row, 3)
        restoring = 4.0 * sum3(lambda m: strain[i][m] * affine[m][j])
        out_ref[RIGHT + row] = weight * get(vel_scr, 3 + row) - STIFFNESS * restoring
        out_ref[AFFINE + row] = affine[i][j]
    for i in range(3):
        out_ref[SHIFT + i] = get(state_scr, i) + get(vel_scr, i)
    out_ref[WEIGHT] = 1.0 / weight


def at_ends():
    bulk = lax.axis_index("bulk")
    return bulk == 0, bulk == lax.axis_size("bulk") - 1


def inner_kernel(
    total_ref, cell_ref, body_ref, count_ref, pos_ref, touch_ref, touch_pos_ref,
    state_ref, vel_ref, mass_ref,
    velocity_ref, sent_ref, first_ref, prepared_ref, state_scr, vel_scr, mass_scr,
):
    prepare(state_ref, vel_ref, mass_ref, prepared_ref, state_scr, vel_scr, mass_scr)
    at_start, at_end = at_ends()
    wall = (iota((LAYERS, COLUMNS), 0) == LAYERS - 1) & at_end
    sums = [total_ref[LAYERS * i : LAYERS * (i + 1)] for i in range(4)]
    mass = sums[0]
    push = []
    for i in range(3):
        velocity = jnp.where(wall, 0.0, sums[i + 1] / (mass + 1.0) + PULL[i])
        velocity_ref[i] = velocity
        push.append(mass * velocity)
    owners = cell_ref.shape[0]
    lanes = iota((owners, LANES), 1)
    counts = jnp.sum(
        jnp.where(iota((owners, owners), 0) == iota((owners, owners), 1), count_ref[...], 0),
        axis=1, keepdims=True,
    )

    def put(row, value):
        put_blocks(sent_ref, row, value, ROWS, owners * OUT // 16)

    for half in range(2):
        part = slice(half * LANES, (half + 1) * LANES)
        cell = cell_ref[:, part]
        live = lanes + half * LANES < counts
        key, index = jnp.where(live, cell >> 7, -1), cell & (LANES - 1)
        found = [jnp.zeros((owners, LANES), f32) for i in range(3)]
        for layer in range(1, LAYERS):
            for side in range(2):
                here = key == 2 * layer + side
                for i in range(3):
                    row = push[i][layer : layer + 1, side * LANES : (side + 1) * LANES]
                    found[i] = jnp.where(here, lane_pick(row, index), found[i])
        for i in range(3):
            put(2 * i + half, found[i])
            put(NODE_POS + 2 * i + half, pos_ref[i, :, part])
        put(NODE_BODY + half, body_ref[:, part].astype(f32))
        first_ref[:, part] = jnp.where(live & (cell < COLUMNS), cell, -1)
    put(TOUCH_BODY, touch_ref[...].astype(f32))
    for i in range(3):
        put(TOUCH_POS + i, touch_pos_ref[i])


def first_kernel(total_ref, cut_ref, ring_ref, inner_ref, begun_ref, first_ref, velocity_ref, sent_ref):
    at_start, at_end = at_ends()
    after_cut = lax.axis_index("bulk") == CUT + 1
    owners = first_ref.shape[0]
    turn = owners * OUT // 16
    sums = [total_ref[LAYERS * i : LAYERS * i + 1] + jnp.where(after_cut, cut_ref[i : i + 1], ring_ref[i : i + 1]) for i in range(4)]
    mass = sums[0]
    velocity_ref[...] = inner_ref[...]
    sent_ref[...] = begun_ref[...]
    push = []
    for i in range(3):
        velocity = jnp.where(at_start, 0.0, sums[i + 1] / (mass + 1.0) + PULL[i])
        velocity_ref[i, 0:1] = velocity
        push.append(mass * velocity)
    for half in range(2):
        cell = first_ref[:, half * LANES : (half + 1) * LANES]
        key, index = cell >> 7, cell & (LANES - 1)
        for i in range(3):
            found = get_blocks(begun_ref, 2 * i + half, owners, ROWS, turn)
            for side in range(2):
                row = push[i][:, side * LANES : (side + 1) * LANES]
                found = jnp.where(key == side, lane_pick(row, index), found)
            put_blocks(sent_ref, 2 * i + half, found, ROWS, turn)


def body_kernel(got_ref, prepared_ref, next_ref, back_ref, next_scr):
    sources = got_ref.shape[0] // ROWS
    pattern = iota((8, LANES), 0)
    quarter, second = pattern & 3, pattern >= 4
    numbers = iota((LANES, LANES), 0)
    sums = jnp.zeros((96, LANES), f32)
    numbers16 = iota((LANES, LANES), 0).astype(f32).astype(bf16)
    for source in range(sources):
        tables, lefts = [], []
        for half in range(2):
            take = lambda row: got_ref[source * ROWS + row : source * ROWS + row + 1, :]
            wide = lambda row: jnp.broadcast_to(take(row), (8, LANES))
            body = take(NODE_BODY + half).astype(i32)
            here = quarter == jnp.broadcast_to(body >> 7, (8, LANES))
            force = [jnp.where(here, wide(2 * i + half), 0.0) for i in range(3)]
            place = [wide(NODE_POS + 2 * i + half) for i in range(3)]
            pick = lambda x, y: jnp.where(second, y, x)
            f01, f12 = pick(force[0], force[1]), pick(force[1], force[2])
            x12, x01, x20 = pick(place[1], place[2]), pick(place[0], place[1]), pick(place[2], place[0])
            blocks = [
                f01, pick(force[2], force[0] * place[0]), force[0] * x12, force[1] * x01, f12 * x20, force[2] * x12,
            ]
            exact = jnp.concatenate(blocks, axis=0)
            coarse = exact.astype(bf16)
            fine = (exact - coarse.astype(f32)).astype(bf16)
            lefts.append(jnp.concatenate([coarse, fine], axis=0))
            low = (body & (LANES - 1)).astype(f32).astype(bf16)
            tables.append(jnp.where(numbers16 == jnp.broadcast_to(low, (LANES, LANES)), bf16(1), bf16(0)))
        sums = sums + rows_dot(jnp.concatenate(lefts, axis=1), jnp.concatenate(tables, axis=1))
    sums = sums[:48] + sums[48:]
    force = [sums[4 * i : 4 * i + 4] for i in range(12)]
    inverse_weight = prepared_ref[WEIGHT]
    result = [prepared_ref[SHIFT + i] + force[i] * inverse_weight for i in range(3)]
    right = [prepared_ref[RIGHT + row] + force[3 + row] for row in range(9)]
    for column in range(9):
        for row in range(column + 1, 9):
            right[row] = right[row] - prepared_ref[lower_at(row, column)] * right[column]
    for column in reversed(range(9)):
        value = right[column] * prepared_ref[INVERSE + column]
        for row in range(column + 1, 9):
            value = value - prepared_ref[lower_at(row, column)] * right[row]
        right[column] = value
    result += [prepared_ref[AFFINE + row] + right[row] for row in range(9)]
    for row in range(12):
        next_scr[8 * row : 8 * row + 4, :] = result[row]
    for part in range(4):
        next_ref[:, part * LANES : (part + 1) * LANES] = next_scr[pl.ds(part, 12, stride=8), :]
    many = lambda row: got_ref[pl.ds(row, sources, stride=ROWS), :]
    body = many(TOUCH_BODY).astype(i32)
    place = [many(TOUCH_POS + i) for i in range(3)]
    key, index = body >> 7, body & (LANES - 1)
    here = [key == part for part in range(1, 4)]

    def pick(row):
        value = lane_pick(result[row][0:1], index)
        for part in range(1, 4):
            value = jnp.where(here[part - 1], lane_pick(result[row][part : part + 1], index), value)
        return value

    for i in range(3):
        point = pick(i)
        for j in range(3):
            point = point + pick(3 + 3 * i + j) * place[j]
        put_blocks(back_ref, i, point, BACK, sources * (HOME - OUT) // 16)


def finish_kernel(points_ref, next_ref, speeds_ref, point_ref, body_ref, velocity_ref):
    body_ref[...] = next_ref[...]
    owners = points_ref.shape[0] // BACK
    for i in range(3):
        point_ref[owners * i : owners * (i + 1), :] = get_blocks(points_ref, i, owners, BACK, owners * HOME // 16)
        for half in range(2):
            velocity_ref[pl.ds(2 * LAYERS * i + half, LAYERS, stride=2), :] = speeds_ref[
                i, :, half * LANES : (half + 1) * LANES
            ]


CUT = 1


def ring_pairs(count):
    return [(i, i + 1) for i in range(count - 1) if i != CUT] + [(CUT, 0), (count - 1, CUT + 1)]


def cut_pairs(count, width):
    pairs = []
    for row in range(count):
        for place in range(width):
            other = {CUT: CUT + 1, CUT + 1: CUT}.get(row)
            to = (row, place ^ 1) if other is None else (other, place)
            pairs.append((row * width + place, to[0] * width + to[1]))
    return pairs


def exchange(blocks, count, turn):
    shaped = blocks.reshape(count, 1, -1)
    moved = lax.all_to_all(
        shaped, "wide", split_axis=0, concat_axis=0, tiled=True,
        axis_index_groups=[group_order(count, turn)],
    )
    return moved.reshape(blocks.shape)


def shape(dims):
    return jax.ShapeDtypeStruct(dims, f32)


def call(kernel, name, out_shape, scratch=(), flops=None):
    def run(*operands):
        cost = flops and pl.CostEstimate(flops=flops, bytes_accessed=1 << 20, transcendentals=0)
        return pl.pallas_call(
            kernel,
            out_shape=out_shape,
            in_specs=[VMEM] * len(operands),
            out_specs=jax.tree.map(lambda x: VMEM, out_shape),
            scratch_shapes=scratch,
            cost_estimate=cost,
            name=name,
            compiler_params=pltpu.CompilerParams(vmem_limit_bytes=8 << 20),
        )(*operands)

    return run


def per_device(
    particle_cell, particle_frac, particle_mass, particle_vel, node_cell, node_body, node_count,
    node_pos, body_state, body_vel, body_mass, touch_body, touch_pos,
):
    owners = lax.axis_size("wide")
    bulks = lax.axis_size("bulk")
    bodies = body_state.shape[1]
    layers = call(
        layers_kernel, "layers", jax.ShapeDtypeStruct((LAYERS, particle_cell.shape[1]), i32), flops=10**9
    )()
    total, ghost = call(
        particles_kernel, "particles", (shape((4 * LAYERS, COLUMNS)), shape((8, COLUMNS))), flops=10**9
    )(layers, particle_cell, particle_frac, particle_mass, particle_vel)
    by_ring = lax.ppermute(ghost, "bulk", ring_pairs(bulks))
    over_cut = lax.ppermute(ghost, ("bulk", "wide"), cut_pairs(bulks, owners))
    held = (
        node_cell, node_body, node_count.reshape(1, -1), node_pos, touch_body, touch_pos,
        body_state, body_vel, body_mass.reshape(1, -1),
    )
    blocks = shape((owners * ROWS, LANES))
    speeds = shape((3, LAYERS, COLUMNS))
    inner, begun, first, prepared = call(
        inner_kernel,
        "inner",
        (speeds, blocks, jax.ShapeDtypeStruct(node_cell.shape, i32), shape((PREPARED, 4, LANES))),
        scratch=[pltpu.VMEM((96, LANES), f32), pltpu.VMEM((96, LANES), f32), pltpu.VMEM((8, LANES), f32)],
        flops=10**9,
    )(total, *held)
    velocity, sent = call(first_kernel, "first", (speeds, blocks))(total, over_cut, by_ring, inner, begun, first)
    got = exchange(sent, owners, owners * OUT // 16)
    body_next, back = call(
        body_kernel, "bodies", (shape((12, bodies)), shape((owners * BACK, LANES))),
        scratch=[pltpu.VMEM((96, LANES), f32)],
    )(got, prepared)
    points = exchange(back, owners, owners * HOME // 16)
    touch_point, body_next, velocity = call(
        finish_kernel, "finish",
        (shape((3 * owners, LANES)), shape((12, bodies)), shape((3 * LAYERS * COLUMNS // LANES, LANES))),
    )(points, body_next, velocity)
    return (
        body_next,
        velocity.reshape(3, LAYERS, 1, COLUMNS),
        touch_point.reshape(3, owners, LANES),
    )


def solution(mesh):
    placed = (
        P(("bulk", "wide"), None),
        P(("bulk", "wide"), None),
        P(("bulk", "wide"), None),
        P(None, ("bulk", "wide"), None),
        P(("bulk", "wide"), None),
        P(("bulk", "wide"), None),
        P(("bulk", "wide")),
        P(None, ("bulk", "wide"), None),
        P(None, ("bulk", "wide")),
        P(None, ("bulk", "wide")),
        P(("bulk", "wide")),
        P(("bulk", "wide"), None),
        P(None, ("bulk", "wide"), None),
    )
    return jax.shard_map(
        per_device,
        mesh=mesh,
        in_specs=placed,
        out_specs=(
            P(None, ("bulk", "wide")),
            P(None, "bulk", "wide", None),
            P(None, ("bulk", "wide"), None),
        ),
        check_vma=False,
    )
```

```python
import functools

import jax
import jax.numpy as jnp
from jax import lax
from jax.experimental import pallas as pl
from jax.experimental.pallas import tpu as pltpu
from jax.sharding import PartitionSpec as P

LAYERS = 16
COLUMNS = 256
LANES = 128
STIFFNESS = 0.05
PULL = (0.0, 0.0, -0.5)
ROWS = 18
NODE_BODY, NODE_POS, TOUCH_BODY, TOUCH_POS = 6, 8, 14, 15
OUT, HOME = 11, 9
BACK = 3

f32, bf16, i32 = jnp.float32, jnp.bfloat16, jnp.int32
VMEM = pl.BlockSpec(memory_space=pltpu.VMEM)


def iota(shape, dim):
    return lax.broadcasted_iota(i32, shape, dim)


def rows_dot(a, b):
    return lax.dot_general(a, b, (((1,), (1,)), ((), ())), preferred_element_type=f32)


def layers_kernel(layers_ref):
    layers_ref[...] = iota(layers_ref.shape, 0)


def particle_values(frac, mass, vel_ref):
    lower = 1.0 - frac
    rounded = lambda x: x.astype(bf16).astype(f32)
    moments = [mass * vel_ref[i] for i in range(3)]
    low = [mass * lower] + [moment * lower for moment in moments]
    high = [mass * frac] + [moment * frac for moment in moments]
    return [rounded(x) for x in low], [rounded(x) for x in high]


def column_table(cell):
    columns = iota((COLUMNS, cell.shape[1]), 0) == (cell & (COLUMNS - 1))
    return jnp.where(columns, 1.0, 0.0).astype(bf16)


def ghost_kernel(layers_ref, cell_ref, frac_ref, mass_ref, vel_ref, ghost_ref):
    cell = cell_ref[...]
    high = particle_values(frac_ref[...], mass_ref[...], vel_ref)[1]
    rows = layers_ref[...]
    left = jnp.zeros(rows.shape, f32)
    for i, x in enumerate(high):
        left = jnp.where((rows == i) & (cell >> 8 == LAYERS - 1), x, left)
    ghost_ref[...] = rows_dot(left.astype(bf16), column_table(cell))[:8]


def layer_sums(layers_ref, cell, frac, mass, vel_ref):
    layer = cell >> 8
    layers = layers_ref[...]
    here, above = layers == layer, layers == layer + 1
    low, high = particle_values(frac, mass, vel_ref)
    blocks = [jnp.where(here, x, 0.0) for x in low] + [jnp.where(above, x, 0.0) for x in high]
    sums = rows_dot(jnp.concatenate(blocks, axis=0).astype(bf16), column_table(cell))
    half = 4 * LAYERS
    return sums[:half] + sums[half:]


def group_order(count, turn):
    return [(i + turn) % count for i in range(count)]


def put_blocks(ref, row, value, rows, turn):
    count = value.shape[0]
    turn = turn % count
    ref[pl.ds(row, count - turn, stride=rows), :] = value[turn:]
    if turn:
        ref[pl.ds((count - turn) * rows + row, turn, stride=rows), :] = value[:turn]


def get_blocks(ref, row, count, rows, turn):
    turn = turn % count
    tail = ref[pl.ds(row, count - turn, stride=rows), :]
    if not turn:
        return tail
    return jnp.concatenate([ref[pl.ds((count - turn) * rows + row, turn, stride=rows), :], tail], axis=0)


def lane_pick(row, index):
    table = jnp.broadcast_to(row, index.shape)
    return jnp.take_along_axis(table, index, axis=1, mode="promise_in_bounds")


def split_rows(source_ref, scratch_ref, rows):
    for part in range(4):
        scratch_ref[pl.ds(part, rows, stride=8), :] = source_ref[:, part * LANES : (part + 1) * LANES]


LOWER, INVERSE, RIGHT, SHIFT, WEIGHT, AFFINE, PREPARED = 0, 36, 45, 54, 57, 58, 67


def lower_at(row, column):
    return LOWER + row * (row - 1) // 2 + column


def prepare(state_ref, vel_ref, mass_ref, out_ref, state_scr, vel_scr, mass_scr):
    split_rows(state_ref, state_scr, 12)
    split_rows(vel_ref, vel_scr, 12)
    split_rows(mass_ref, mass_scr, 1)
    get = lambda ref, row: ref[8 * row : 8 * row + 4, :]
    weight = get(mass_scr, 0)
    affine = [[get(state_scr, 3 + 3 * i + j) for j in range(3)] for i in range(3)]
    sum3 = lambda f: f(0) + f(1) + f(2)
    strain = [[None] * 3 for i in range(3)]
    gram = [[None] * 3 for i in range(3)]
    for i in range(3):
        for j in range(i, 3):
            value = sum3(lambda m: affine[i][m] * affine[j][m])
            strain[i][j] = strain[j][i] = value - 1.0 if i == j else value
            gram[i][j] = gram[j][i] = sum3(lambda m: affine[m][i] * affine[m][j])
    matrix = [[None] * 9 for i in range(9)]
    for row in range(9):
        i, j = divmod(row, 3)
        for column in range(row + 1):
            k, l = divmod(column, 3)
            value = affine[i][l] * affine[k][j]
            if i == k:
                value = gram[l][j] + value
            if j == l:
                value = value + strain[i][k]
            value = (4.0 * STIFFNESS) * value
            matrix[row][column] = value + weight if row == column else value
    for column in range(9):
        inverse = 1.0 / matrix[column][column]
        out_ref[INVERSE + column] = inverse
        factors = {}
        for row in range(column + 1, 9):
            factors[row] = matrix[row][column] * inverse
            out_ref[lower_at(row, column)] = factors[row]
        for row in range(column + 1, 9):
            for other in range(column + 1, row + 1):
                matrix[row][other] = matrix[row][other] - factors[row] * matrix[other][column]
    for row in range(9):
        i, j = divmod(row, 3)
        restoring = 4.0 * sum3(lambda m: strain[i][m] * affine[m][j])
        out_ref[RIGHT + row] = weight * get(vel_scr, 3 + row) - STIFFNESS * restoring
        out_ref[AFFINE + row] = affine[i][j]
    for i in range(3):
        out_ref[SHIFT + i] = get(state_scr, i) + get(vel_scr, i)
    out_ref[WEIGHT] = 1.0 / weight


def at_ends():
    bulk = lax.axis_index("bulk")
    return bulk == 0, bulk == lax.axis_size("bulk") - 1


def inner_kernel(
    layers_ref, particle_ref, frac_ref, particle_mass_ref, particle_vel_ref,
    cell_ref, body_ref, count_ref, pos_ref, touch_ref, touch_pos_ref,
    state_ref, vel_ref, mass_ref,
    total_ref, velocity_ref, sent_ref, first_ref, prepared_ref, state_scr, vel_scr, mass_scr,
):
    prepare(state_ref, vel_ref, mass_ref, prepared_ref, state_scr, vel_scr, mass_scr)
    at_start, at_end = at_ends()
    wall = (iota((LAYERS, COLUMNS), 0) == LAYERS - 1) & at_end
    total = layer_sums(layers_ref, particle_ref[...], frac_ref[...], particle_mass_ref[...], particle_vel_ref)
    total_ref[...] = total
    sums = [total[LAYERS * i : LAYERS * (i + 1)] for i in range(4)]
    mass = sums[0]
    push = []
    for i in range(3):
        velocity = jnp.where(wall, 0.0, sums[i + 1] / (mass + 1.0) + PULL[i])
        velocity_ref[i] = velocity
        push.append(mass * velocity)
    owners = cell_ref.shape[0]
    lanes = iota((owners, LANES), 1)
    counts = jnp.sum(
        jnp.where(iota((owners, owners), 0) == iota((owners, owners), 1), count_ref[...], 0),
        axis=1, keepdims=True,
    )

    def put(row, value):
        put_blocks(sent_ref, row, value, ROWS, owners * OUT // 16)

    for half in range(2):
        part = slice(half * LANES, (half + 1) * LANES)
        cell = cell_ref[:, part]
        live = lanes + half * LANES < counts
        key, index = jnp.where(live, cell >> 7, -1), cell & (LANES - 1)
        found = [jnp.zeros((owners, LANES), f32) for i in range(3)]
        for layer in range(1, LAYERS):
            for side in range(2):
                here = key == 2 * layer + side
                for i in range(3):
                    row = push[i][layer : layer + 1, side * LANES : (side + 1) * LANES]
                    found[i] = jnp.where(here, lane_pick(row, index), found[i])
        for i in range(3):
            put(2 * i + half, found[i])
            put(NODE_POS + 2 * i + half, pos_ref[i, :, part])
        put(NODE_BODY + half, body_ref[:, part].astype(f32))
        first_ref[:, part] = jnp.where(live & (cell < COLUMNS), cell, -1)
    put(TOUCH_BODY, touch_ref[...].astype(f32))
    for i in range(3):
        put(TOUCH_POS + i, touch_pos_ref[i])


def first_kernel(total_ref, cut_ref, ring_ref, inner_ref, begun_ref, first_ref, velocity_ref, sent_ref):
    at_start, at_end = at_ends()
    after_cut = lax.axis_index("bulk") == CUT + 1
    owners = first_ref.shape[0]
    turn = owners * OUT // 16
    sums = [total_ref[LAYERS * i : LAYERS * i + 1] + jnp.where(after_cut, cut_ref[i : i + 1], ring_ref[i : i + 1]) for i in range(4)]
    mass = sums[0]
    velocity_ref[...] = inner_ref[...]
    sent_ref[...] = begun_ref[...]
    push = []
    for i in range(3):
        velocity = jnp.where(at_start, 0.0, sums[i + 1] / (mass + 1.0) + PULL[i])
        velocity_ref[i, 0:1] = velocity
        push.append(mass * velocity)
    for half in range(2):
        cell = first_ref[:, half * LANES : (half + 1) * LANES]
        key, index = cell >> 7, cell & (LANES - 1)
        for i in range(3):
            found = get_blocks(begun_ref, 2 * i + half, owners, ROWS, turn)
            for side in range(2):
                row = push[i][:, side * LANES : (side + 1) * LANES]
                found = jnp.where(key == side, lane_pick(row, index), found)
            put_blocks(sent_ref, 2 * i + half, found, ROWS, turn)


def body_kernel(got_ref, prepared_ref, next_ref, back_ref, next_scr):
    sources = got_ref.shape[0] // ROWS
    pattern = iota((8, LANES), 0)
    quarter, second = pattern & 3, pattern >= 4
    numbers = iota((LANES, LANES), 0)
    sums = jnp.zeros((96, LANES), f32)
    numbers16 = iota((LANES, LANES), 0).astype(f32).astype(bf16)
    for source in range(sources):
        tables, lefts = [], []
        for half in range(2):
            take = lambda row: got_ref[source * ROWS + row : source * ROWS + row + 1, :]
            wide = lambda row: jnp.broadcast_to(take(row), (8, LANES))
            body = take(NODE_BODY + half).astype(i32)
            here = quarter == jnp.broadcast_to(body >> 7, (8, LANES))
            force = [jnp.where(here, wide(2 * i + half), 0.0) for i in range(3)]
            place = [wide(NODE_POS + 2 * i + half) for i in range(3)]
            pick = lambda x, y: jnp.where(second, y, x)
            f01, f12 = pick(force[0], force[1]), pick(force[1], force[2])
            x12, x01, x20 = pick(place[1], place[2]), pick(place[0], place[1]), pick(place[2], place[0])
            blocks = [
                f01, pick(force[2], force[0] * place[0]), force[0] * x12, force[1] * x01, f12 * x20, force[2] * x12,
            ]
            exact = jnp.concatenate(blocks, axis=0)
            coarse = exact.astype(bf16)
            fine = (exact - coarse.astype(f32)).astype(bf16)
            lefts.append(jnp.concatenate([coarse, fine], axis=0))
            low = (body & (LANES - 1)).astype(f32).astype(bf16)
            tables.append(jnp.where(numbers16 == jnp.broadcast_to(low, (LANES, LANES)), bf16(1), bf16(0)))
        sums = sums + rows_dot(jnp.concatenate(lefts, axis=1), jnp.concatenate(tables, axis=1))
    sums = sums[:48] + sums[48:]
    force = [sums[4 * i : 4 * i + 4] for i in range(12)]
    inverse_weight = prepared_ref[WEIGHT]
    result = [prepared_ref[SHIFT + i] + force[i] * inverse_weight for i in range(3)]
    right = [prepared_ref[RIGHT + row] + force[3 + row] for row in range(9)]
    for column in range(9):
        for row in range(column + 1, 9):
            right[row] = right[row] - prepared_ref[lower_at(row, column)] * right[column]
    for column in reversed(range(9)):
        value = right[column] * prepared_ref[INVERSE + column]
        for row in range(column + 1, 9):
            value = value - prepared_ref[lower_at(row, column)] * right[row]
        right[column] = value
    result += [prepared_ref[AFFINE + row] + right[row] for row in range(9)]
    for row in range(12):
        next_scr[8 * row : 8 * row + 4, :] = result[row]
    for part in range(4):
        next_ref[:, part * LANES : (part + 1) * LANES] = next_scr[pl.ds(part, 12, stride=8), :]
    many = lambda row: got_ref[pl.ds(row, sources, stride=ROWS), :]
    body = many(TOUCH_BODY).astype(i32)
    place = [many(TOUCH_POS + i) for i in range(3)]
    key, index = body >> 7, body & (LANES - 1)
    here = [key == part for part in range(1, 4)]

    def pick(row):
        value = lane_pick(result[row][0:1], index)
        for part in range(1, 4):
            value = jnp.where(here[part - 1], lane_pick(result[row][part : part + 1], index), value)
        return value

    for i in range(3):
        point = pick(i)
        for j in range(3):
            point = point + pick(3 + 3 * i + j) * place[j]
        put_blocks(back_ref, i, point, BACK, sources * (HOME - OUT) // 16)


def finish_kernel(points_ref, next_ref, speeds_ref, point_ref, body_ref, velocity_ref):
    body_ref[...] = next_ref[...]
    owners = points_ref.shape[0] // BACK
    for i in range(3):
        point_ref[owners * i : owners * (i + 1), :] = get_blocks(points_ref, i, owners, BACK, owners * HOME // 16)
        for half in range(2):
            velocity_ref[pl.ds(2 * LAYERS * i + half, LAYERS, stride=2), :] = speeds_ref[
                i, :, half * LANES : (half + 1) * LANES
            ]


CUT = 1


def ring_pairs(count):
    return [(i, i + 1) for i in range(count - 1) if i != CUT] + [(CUT, 0), (count - 1, CUT + 1)]


def cut_pairs(count, width):
    pairs = []
    for row in range(count):
        for place in range(width):
            other = {CUT: CUT + 1, CUT + 1: CUT}.get(row)
            to = (row, place ^ 1) if other is None else (other, place)
            pairs.append((row * width + place, to[0] * width + to[1]))
    return pairs


def exchange(blocks, count, turn):
    shaped = blocks.reshape(count, 1, -1)
    moved = lax.all_to_all(
        shaped, "wide", split_axis=0, concat_axis=0, tiled=True,
        axis_index_groups=[group_order(count, turn)],
    )
    return moved.reshape(blocks.shape)


def shape(dims):
    return jax.ShapeDtypeStruct(dims, f32)


def call(kernel, name, out_shape, scratch=(), flops=None):
    def run(*operands):
        cost = flops and pl.CostEstimate(flops=flops, bytes_accessed=1 << 20, transcendentals=0)
        return pl.pallas_call(
            kernel,
            out_shape=out_shape,
            in_specs=[VMEM] * len(operands),
            out_specs=jax.tree.map(lambda x: VMEM, out_shape),
            scratch_shapes=scratch,
            cost_estimate=cost,
            name=name,
            compiler_params=pltpu.CompilerParams(vmem_limit_bytes=8 << 20),
        )(*operands)

    return run


def per_device(
    particle_cell, particle_frac, particle_mass, particle_vel, node_cell, node_body, node_count,
    node_pos, body_state, body_vel, body_mass, touch_body, touch_pos,
):
    owners = lax.axis_size("wide")
    bulks = lax.axis_size("bulk")
    bodies = body_state.shape[1]
    layers = call(
        layers_kernel, "layers", jax.ShapeDtypeStruct((LAYERS, particle_cell.shape[1]), i32), flops=10**9
    )()
    particles = (layers, particle_cell, particle_frac, particle_mass, particle_vel)
    ghost = call(ghost_kernel, "ghost", shape((8, COLUMNS)), flops=10**9)(*particles)
    by_ring = lax.ppermute(ghost, "bulk", ring_pairs(bulks))
    over_cut = lax.ppermute(ghost, ("bulk", "wide"), cut_pairs(bulks, owners))
    held = (
        node_cell, node_body, node_count.reshape(1, -1), node_pos, touch_body, touch_pos,
        body_state, body_vel, body_mass.reshape(1, -1),
    )
    blocks = shape((owners * ROWS, LANES))
    speeds = shape((3, LAYERS, COLUMNS))
    total, inner, begun, first, prepared = call(
        inner_kernel,
        "inner",
        (
            shape((4 * LAYERS, COLUMNS)), speeds, blocks, jax.ShapeDtypeStruct(node_cell.shape, i32),
            shape((PREPARED, 4, LANES)),
        ),
        scratch=[pltpu.VMEM((96, LANES), f32), pltpu.VMEM((96, LANES), f32), pltpu.VMEM((8, LANES), f32)],
        flops=10**9,
    )(*particles, *held)
    velocity, sent = call(first_kernel, "first", (speeds, blocks))(total, over_cut, by_ring, inner, begun, first)
    got = exchange(sent, owners, owners * OUT // 16)
    body_next, back = call(
        body_kernel, "bodies", (shape((12, bodies)), shape((owners * BACK, LANES))),
        scratch=[pltpu.VMEM((96, LANES), f32)],
    )(got, prepared)
    points = exchange(back, owners, owners * HOME // 16)
    touch_point, body_next, velocity = call(
        finish_kernel, "finish",
        (shape((3 * owners, LANES)), shape((12, bodies)), shape((3 * LAYERS * COLUMNS // LANES, LANES))),
    )(points, body_next, velocity)
    return (
        body_next,
        velocity.reshape(3, LAYERS, 1, COLUMNS),
        touch_point.reshape(3, owners, LANES),
    )


def solution(mesh):
    placed = (
        P(("bulk", "wide"), None),
        P(("bulk", "wide"), None),
        P(("bulk", "wide"), None),
        P(None, ("bulk", "wide"), None),
        P(("bulk", "wide"), None),
        P(("bulk", "wide"), None),
        P(("bulk", "wide")),
        P(None, ("bulk", "wide"), None),
        P(None, ("bulk", "wide")),
        P(None, ("bulk", "wide")),
        P(("bulk", "wide")),
        P(("bulk", "wide"), None),
        P(None, ("bulk", "wide"), None),
    )
    return jax.shard_map(
        per_device,
        mesh=mesh,
        in_specs=placed,
        out_specs=(
            P(None, ("bulk", "wide")),
            P(None, "bulk", "wide", None),
            P(None, ("bulk", "wide"), None),
        ),
        check_vma=False,
    )
```

```python
import functools

import jax
import jax.numpy as jnp
from jax import lax
from jax.experimental import pallas as pl
from jax.experimental.pallas import tpu as pltpu
from jax.sharding import PartitionSpec as P

LAYERS = 16
COLUMNS = 256
LANES = 128
STIFFNESS = 0.05
PULL = (0.0, 0.0, -0.5)
ROWS = 18
NODE_BODY, NODE_POS, TOUCH_BODY, TOUCH_POS = 6, 8, 14, 15
OUT, HOME = 11, 9
BACK = 3

f32, bf16, i32 = jnp.float32, jnp.bfloat16, jnp.int32
VMEM = pl.BlockSpec(memory_space=pltpu.VMEM)


def iota(shape, dim):
    return lax.broadcasted_iota(i32, shape, dim)


def rows_dot(a, b):
    return lax.dot_general(a, b, (((1,), (1,)), ((), ())), preferred_element_type=f32)


def layers_kernel(layers_ref):
    layers_ref[...] = iota(layers_ref.shape, 0)


def particle_values(frac, mass, vel_ref):
    lower = 1.0 - frac
    rounded = lambda x: x.astype(bf16).astype(f32)
    moments = [mass * vel_ref[i] for i in range(3)]
    low = [mass * lower] + [moment * lower for moment in moments]
    high = [mass * frac] + [moment * frac for moment in moments]
    return [rounded(x) for x in low], [rounded(x) for x in high]


def column_table(cell):
    shape_ = (COLUMNS, cell.shape[1])
    column = (cell & (COLUMNS - 1)).astype(f32).astype(bf16)
    columns = iota(shape_, 0).astype(f32).astype(bf16)
    return jnp.where(columns == jnp.broadcast_to(column, shape_), bf16(1), bf16(0))


def ghost_kernel(layers_ref, cell_ref, frac_ref, mass_ref, vel_ref, ghost_ref):
    cell = cell_ref[...]
    high = particle_values(frac_ref[...], mass_ref[...], vel_ref)[1]
    rows = layers_ref[...]
    left = jnp.zeros(rows.shape, f32)
    for i, x in enumerate(high):
        left = jnp.where((rows == i) & (cell >> 8 == LAYERS - 1), x, left)
    ghost_ref[...] = rows_dot(left.astype(bf16), column_table(cell))[:8]


def layer_sums(layers_ref, cell, frac, mass, vel_ref):
    layer = cell >> 8
    layers = layers_ref[...]
    here, above = layers == layer, layers == layer + 1
    low, high = particle_values(frac, mass, vel_ref)
    blocks = [jnp.where(here, x, 0.0) for x in low] + [jnp.where(above, x, 0.0) for x in high]
    sums = rows_dot(jnp.concatenate(blocks, axis=0).astype(bf16), column_table(cell))
    half = 4 * LAYERS
    return sums[:half] + sums[half:]


def group_order(count, turn):
    return [(i + turn) % count for i in range(count)]


def put_blocks(ref, row, value, rows, turn):
    count = value.shape[0]
    turn = turn % count
    ref[pl.ds(row, count - turn, stride=rows), :] = value[turn:]
    if turn:
        ref[pl.ds((count - turn) * rows + row, turn, stride=rows), :] = value[:turn]


def get_blocks(ref, row, count, rows, turn):
    turn = turn % count
    tail = ref[pl.ds(row, count - turn, stride=rows), :]
    if not turn:
        return tail
    return jnp.concatenate([ref[pl.ds((count - turn) * rows + row, turn, stride=rows), :], tail], axis=0)


def lane_pick(row, index):
    table = jnp.broadcast_to(row, index.shape)
    return jnp.take_along_axis(table, index, axis=1, mode="promise_in_bounds")


def split_rows(source_ref, scratch_ref, rows):
    for part in range(4):
        scratch_ref[pl.ds(part, rows, stride=8), :] = source_ref[:, part * LANES : (part + 1) * LANES]


LOWER, INVERSE, RIGHT, SHIFT, WEIGHT, AFFINE, PREPARED = 0, 36, 45, 54, 57, 58, 67


def lower_at(row, column):
    return LOWER + row * (row - 1) // 2 + column


def prepare(state_ref, vel_ref, mass_ref, out_ref, state_scr, vel_scr, mass_scr):
    split_rows(state_ref, state_scr, 12)
    split_rows(vel_ref, vel_scr, 12)
    split_rows(mass_ref, mass_scr, 1)
    get = lambda ref, row: ref[8 * row : 8 * row + 4, :]
    weight = get(mass_scr, 0)
    affine = [[get(state_scr, 3 + 3 * i + j) for j in range(3)] for i in range(3)]
    sum3 = lambda f: f(0) + f(1) + f(2)
    strain = [[None] * 3 for i in range(3)]
    gram = [[None] * 3 for i in range(3)]
    for i in range(3):
        for j in range(i, 3):
            value = sum3(lambda m: affine[i][m] * affine[j][m])
            strain[i][j] = strain[j][i] = value - 1.0 if i == j else value
            gram[i][j] = gram[j][i] = sum3(lambda m: affine[m][i] * affine[m][j])
    matrix = [[None] * 9 for i in range(9)]
    for row in range(9):
        i, j = divmod(row, 3)
        for column in range(row + 1):
            k, l = divmod(column, 3)
            value = affine[i][l] * affine[k][j]
            if i == k:
                value = gram[l][j] + value
            if j == l:
                value = value + strain[i][k]
            value = (4.0 * STIFFNESS) * value
            matrix[row][column] = value + weight if row == column else value
    for column in range(9):
        inverse = 1.0 / matrix[column][column]
        out_ref[INVERSE + column] = inverse
        factors = {}
        for row in range(column + 1, 9):
            factors[row] = matrix[row][column] * inverse
            out_ref[lower_at(row, column)] = factors[row]
        for row in range(column + 1, 9):
            for other in range(column + 1, row + 1):
                matrix[row][other] = matrix[row][other] - factors[row] * matrix[other][column]
    for row in range(9):
        i, j = divmod(row, 3)
        restoring = 4.0 * sum3(lambda m: strain[i][m] * affine[m][j])
        out_ref[RIGHT + row] = weight * get(vel_scr, 3 + row) - STIFFNESS * restoring
        out_ref[AFFINE + row] = affine[i][j]
    for i in range(3):
        out_ref[SHIFT + i] = get(state_scr, i) + get(vel_scr, i)
    out_ref[WEIGHT] = 1.0 / weight


def at_ends():
    bulk = lax.axis_index("bulk")
    return bulk == 0, bulk == lax.axis_size("bulk") - 1


def inner_kernel(
    layers_ref, particle_ref, frac_ref, particle_mass_ref, particle_vel_ref,
    cell_ref, body_ref, count_ref, pos_ref, touch_ref, touch_pos_ref,
    state_ref, vel_ref, mass_ref,
    total_ref, velocity_ref, sent_ref, first_ref, prepared_ref, state_scr, vel_scr, mass_scr,
):
    prepare(state_ref, vel_ref, mass_ref, prepared_ref, state_scr, vel_scr, mass_scr)
    at_start, at_end = at_ends()
    wall = (iota((LAYERS, COLUMNS), 0) == LAYERS - 1) & at_end
    total = layer_sums(layers_ref, particle_ref[...], frac_ref[...], particle_mass_ref[...], particle_vel_ref)
    total_ref[...] = total
    sums = [total[LAYERS * i : LAYERS * (i + 1)] for i in range(4)]
    mass = sums[0]
    push = []
    for i in range(3):
        velocity = jnp.where(wall, 0.0, sums[i + 1] / (mass + 1.0) + PULL[i])
        velocity_ref[i] = velocity
        push.append(mass * velocity)
    owners = cell_ref.shape[0]
    lanes = iota((owners, LANES), 1)
    counts = jnp.sum(
        jnp.where(iota((owners, owners), 0) == iota((owners, owners), 1), count_ref[...], 0),
        axis=1, keepdims=True,
    )

    def put(row, value):
        put_blocks(sent_ref, row, value, ROWS, owners * OUT // 16)

    for half in range(2):
        part = slice(half * LANES, (half + 1) * LANES)
        cell = cell_ref[:, part]
        live = lanes + half * LANES < counts
        key, index = jnp.where(live, cell >> 7, -1), cell & (LANES - 1)
        found = [jnp.zeros((owners, LANES), f32) for i in range(3)]
        for layer in range(1, LAYERS):
            for side in range(2):
                here = key == 2 * layer + side
                for i in range(3):
                    row = push[i][layer : layer + 1, side * LANES : (side + 1) * LANES]
                    found[i] = jnp.where(here, lane_pick(row, index), found[i])
        for i in range(3):
            put(2 * i + half, found[i])
            put(NODE_POS + 2 * i + half, pos_ref[i, :, part])
        put(NODE_BODY + half, body_ref[:, part].astype(f32))
        first_ref[:, part] = jnp.where(live & (cell < COLUMNS), cell, -1)
    put(TOUCH_BODY, touch_ref[...].astype(f32))
    for i in range(3):
        put(TOUCH_POS + i, touch_pos_ref[i])


def first_kernel(total_ref, cut_ref, ring_ref, inner_ref, begun_ref, first_ref, velocity_ref, sent_ref):
    at_start, at_end = at_ends()
    after_cut = lax.axis_index("bulk") == CUT + 1
    owners = first_ref.shape[0]
    turn = owners * OUT // 16
    sums = [total_ref[LAYERS * i : LAYERS * i + 1] + jnp.where(after_cut, cut_ref[i : i + 1], ring_ref[i : i + 1]) for i in range(4)]
    mass = sums[0]
    velocity_ref[...] = inner_ref[...]
    sent_ref[...] = begun_ref[...]
    push = []
    for i in range(3):
        velocity = jnp.where(at_start, 0.0, sums[i + 1] / (mass + 1.0) + PULL[i])
        velocity_ref[i, 0:1] = velocity
        push.append(mass * velocity)
    for half in range(2):
        cell = first_ref[:, half * LANES : (half + 1) * LANES]
        key, index = cell >> 7, cell & (LANES - 1)
        for i in range(3):
            found = get_blocks(begun_ref, 2 * i + half, owners, ROWS, turn)
            for side in range(2):
                row = push[i][:, side * LANES : (side + 1) * LANES]
                found = jnp.where(key == side, lane_pick(row, index), found)
            put_blocks(sent_ref, 2 * i + half, found, ROWS, turn)


def body_kernel(got_ref, prepared_ref, next_ref, back_ref, next_scr):
    sources = got_ref.shape[0] // ROWS
    pattern = iota((8, LANES), 0)
    quarter, second = pattern & 3, pattern >= 4
    numbers = iota((LANES, LANES), 0)
    sums = jnp.zeros((96, LANES), f32)
    numbers16 = iota((LANES, LANES), 0).astype(f32).astype(bf16)
    for source in range(sources):
        tables, lefts = [], []
        for half in range(2):
            take = lambda row: got_ref[source * ROWS + row : source * ROWS + row + 1, :]
            wide = lambda row: jnp.broadcast_to(take(row), (8, LANES))
            body = take(NODE_BODY + half).astype(i32)
            here = quarter == jnp.broadcast_to(body >> 7, (8, LANES))
            force = [jnp.where(here, wide(2 * i + half), 0.0) for i in range(3)]
            place = [wide(NODE_POS + 2 * i + half) for i in range(3)]
            pick = lambda x, y: jnp.where(second, y, x)
            f01, f12 = pick(force[0], force[1]), pick(force[1], force[2])
            x12, x01, x20 = pick(place[1], place[2]), pick(place[0], place[1]), pick(place[2], place[0])
            blocks = [
                f01, pick(force[2], force[0] * place[0]), force[0] * x12, force[1] * x01, f12 * x20, force[2] * x12,
            ]
            exact = jnp.concatenate(blocks, axis=0)
            coarse = exact.astype(bf16)
            fine = (exact - coarse.astype(f32)).astype(bf16)
            lefts.append(jnp.concatenate([coarse, fine], axis=0))
            low = (body & (LANES - 1)).astype(f32).astype(bf16)
            tables.append(jnp.where(numbers16 == jnp.broadcast_to(low, (LANES, LANES)), bf16(1), bf16(0)))
        sums = sums + rows_dot(jnp.concatenate(lefts, axis=1), jnp.concatenate(tables, axis=1))
    sums = sums[:48] + sums[48:]
    force = [sums[4 * i : 4 * i + 4] for i in range(12)]
    inverse_weight = prepared_ref[WEIGHT]
    result = [prepared_ref[SHIFT + i] + force[i] * inverse_weight for i in range(3)]
    right = [prepared_ref[RIGHT + row] + force[3 + row] for row in range(9)]
    for column in range(9):
        for row in range(column + 1, 9):
            right[row] = right[row] - prepared_ref[lower_at(row, column)] * right[column]
    for column in reversed(range(9)):
        value = right[column] * prepared_ref[INVERSE + column]
        for row in range(column + 1, 9):
            value = value - prepared_ref[lower_at(row, column)] * right[row]
        right[column] = value
    result += [prepared_ref[AFFINE + row] + right[row] for row in range(9)]
    for row in range(12):
        next_scr[8 * row : 8 * row + 4, :] = result[row]
    for part in range(4):
        next_ref[:, part * LANES : (part + 1) * LANES] = next_scr[pl.ds(part, 12, stride=8), :]
    many = lambda row: got_ref[pl.ds(row, sources, stride=ROWS), :]
    body = many(TOUCH_BODY).astype(i32)
    place = [many(TOUCH_POS + i) for i in range(3)]
    key, index = body >> 7, body & (LANES - 1)
    here = [key == part for part in range(1, 4)]

    def pick(row):
        value = lane_pick(result[row][0:1], index)
        for part in range(1, 4):
            value = jnp.where(here[part - 1], lane_pick(result[row][part : part + 1], index), value)
        return value

    for i in range(3):
        point = pick(i)
        for j in range(3):
            point = point + pick(3 + 3 * i + j) * place[j]
        put_blocks(back_ref, i, point, BACK, sources * (HOME - OUT) // 16)


def finish_kernel(points_ref, next_ref, speeds_ref, point_ref, body_ref, velocity_ref):
    body_ref[...] = next_ref[...]
    owners = points_ref.shape[0] // BACK
    for i in range(3):
        point_ref[owners * i : owners * (i + 1), :] = get_blocks(points_ref, i, owners, BACK, owners * HOME // 16)
        for half in range(2):
            velocity_ref[pl.ds(2 * LAYERS * i + half, LAYERS, stride=2), :] = speeds_ref[
                i, :, half * LANES : (half + 1) * LANES
            ]


CUT = 1


def ring_pairs(count):
    return [(i, i + 1) for i in range(count - 1) if i != CUT] + [(CUT, 0), (count - 1, CUT + 1)]


def cut_pairs(count, width):
    pairs = []
    for row in range(count):
        for place in range(width):
            other = {CUT: CUT + 1, CUT + 1: CUT}.get(row)
            to = (row, place ^ 1) if other is None else (other, place)
            pairs.append((row * width + place, to[0] * width + to[1]))
    return pairs


def exchange(blocks, count, turn):
    shaped = blocks.reshape(count, 1, -1)
    moved = lax.all_to_all(
        shaped, "wide", split_axis=0, concat_axis=0, tiled=True,
        axis_index_groups=[group_order(count, turn)],
    )
    return moved.reshape(blocks.shape)


def shape(dims):
    return jax.ShapeDtypeStruct(dims, f32)


def call(kernel, name, out_shape, scratch=(), flops=None):
    def run(*operands):
        cost = flops and pl.CostEstimate(flops=flops, bytes_accessed=1 << 20, transcendentals=0)
        return pl.pallas_call(
            kernel,
            out_shape=out_shape,
            in_specs=[VMEM] * len(operands),
            out_specs=jax.tree.map(lambda x: VMEM, out_shape),
            scratch_shapes=scratch,
            cost_estimate=cost,
            name=name,
            compiler_params=pltpu.CompilerParams(vmem_limit_bytes=8 << 20),
        )(*operands)

    return run


def per_device(
    particle_cell, particle_frac, particle_mass, particle_vel, node_cell, node_body, node_count,
    node_pos, body_state, body_vel, body_mass, touch_body, touch_pos,
):
    owners = lax.axis_size("wide")
    bulks = lax.axis_size("bulk")
    bodies = body_state.shape[1]
    layers = call(
        layers_kernel, "layers", jax.ShapeDtypeStruct((LAYERS, particle_cell.shape[1]), i32), flops=10**9
    )()
    particles = (layers, particle_cell, particle_frac, particle_mass, particle_vel)
    ghost = call(ghost_kernel, "ghost", shape((8, COLUMNS)), flops=10**9)(*particles)
    by_ring = lax.ppermute(ghost, "bulk", ring_pairs(bulks))
    over_cut = lax.ppermute(ghost, ("bulk", "wide"), cut_pairs(bulks, owners))
    held = (
        node_cell, node_body, node_count.reshape(1, -1), node_pos, touch_body, touch_pos,
        body_state, body_vel, body_mass.reshape(1, -1),
    )
    blocks = shape((owners * ROWS, LANES))
    speeds = shape((3, LAYERS, COLUMNS))
    total, inner, begun, first, prepared = call(
        inner_kernel,
        "inner",
        (
            shape((4 * LAYERS, COLUMNS)), speeds, blocks, jax.ShapeDtypeStruct(node_cell.shape, i32),
            shape((PREPARED, 4, LANES)),
        ),
        scratch=[pltpu.VMEM((96, LANES), f32), pltpu.VMEM((96, LANES), f32), pltpu.VMEM((8, LANES), f32)],
        flops=10**9,
    )(*particles, *held)
    velocity, sent = call(first_kernel, "first", (speeds, blocks))(total, over_cut, by_ring, inner, begun, first)
    got = exchange(sent, owners, owners * OUT // 16)
    body_next, back = call(
        body_kernel, "bodies", (shape((12, bodies)), shape((owners * BACK, LANES))),
        scratch=[pltpu.VMEM((96, LANES), f32)],
    )(got, prepared)
    points = exchange(back, owners, owners * HOME // 16)
    touch_point, body_next, velocity = call(
        finish_kernel, "finish",
        (shape((3 * owners, LANES)), shape((12, bodies)), shape((3 * LAYERS * COLUMNS // LANES, LANES))),
    )(points, body_next, velocity)
    return (
        body_next,
        velocity.reshape(3, LAYERS, 1, COLUMNS),
        touch_point.reshape(3, owners, LANES),
    )


def solution(mesh):
    placed = (
        P(("bulk", "wide"), None),
        P(("bulk", "wide"), None),
        P(("bulk", "wide"), None),
        P(None, ("bulk", "wide"), None),
        P(("bulk", "wide"), None),
        P(("bulk", "wide"), None),
        P(("bulk", "wide")),
        P(None, ("bulk", "wide"), None),
        P(None, ("bulk", "wide")),
        P(None, ("bulk", "wide")),
        P(("bulk", "wide")),
        P(("bulk", "wide"), None),
        P(None, ("bulk", "wide"), None),
    )
    return jax.shard_map(
        per_device,
        mesh=mesh,
        in_specs=placed,
        out_specs=(
            P(None, ("bulk", "wide")),
            P(None, "bulk", "wide", None),
            P(None, ("bulk", "wide"), None),
        ),
        check_vma=False,
    )
```
